128 devices in a mesh: gz: 16 (over z, x), gx: 8 (over y, core).
Axes of the slice: x: 4, y: 4, z: 4, core: 2. Of those that a mesh axis runs over, the one named last changes fastest.
Arguments:
- atom_velocity: float32 [3, 16384, 128], P(None, ('gz', 'gx')), may hold values from -4.2 to 4.2
- atom_noise: float32 [3, 16384, 128], P(None, ('gz', 'gx')), may hold values from -6 to 6
- atom_plane: int32 [16384, 128], P(('gz', 'gx')), may hold values from 0 to 255, as said below
- atom_column: int32 [16384, 128], P(('gz', 'gx')), may hold values from 0 to 4095
- brick_count: int32 [16384], P(('gz', 'gx')), may hold values from 32 to 128, as said below
- electron_temp: float32 [256, 128, 256], P('gz', 'gx'), may hold values from 0.05 to 3.8
Outputs:
- new_temp: float32 [256, 128, 256], P('gz', 'gx')
- new_velocity: float32 [3, 16384, 128], P(None, ('gz', 'gx'))
The draws below stay inside these ranges and needn't reach their ends.
Inputs may be any that keep to these rules, and one draw needn't show every extreme that they name: `atom_plane`: all 128 entries of a brick lie in one slab of 16 planes (the planes of one gz index). No slab holds more than 16 bricks of one device, and in every draw one slab holds exactly 16 bricks of every device. `brick_count`: every device holds a brick with 128 used slots.
All inputs are finite; a program needn't handle non-finite values.
Results may differ from the reference program's by a relative error of at most 0.00035.
Values sent between devices are 32-bit elements; how exact they have to be, the bound alone decides.
A program may use at most 128 MiB of HBM per device.

```python
import math
import jax
import jax.numpy as jnp
from jax import lax

CZ = 16
CX = 16
NY = 256
BRICK_DEV = 128
ROW_ATOMS = 128
NZ = 256
NX = 128
BRICKS = 16384
N_GX = 8


def hot_slab_index(key):
    return jax.random.randint(jax.random.fold_in(key, 5), (), 0, NZ // CZ)


def draw_atom_plane(key, part):
    slab_count = NZ // CZ
    device_count = BRICKS // BRICK_DEV
    slot_count = 2 * BRICK_DEV // slab_count
    hot_slab = hot_slab_index(key)
    key_rotation = jax.random.fold_in(jax.random.fold_in(key, 11), 1)
    key_order = jax.random.fold_in(jax.random.fold_in(key, 11), 2)
    key_plane = jax.random.fold_in(jax.random.fold_in(key, 11), 3)
    rotation = jax.random.randint(key_rotation, (device_count, 1), 0, slab_count - 1)
    position = jnp.arange(BRICK_DEV, dtype=jnp.int32)[None, :]
    others = (hot_slab + 1 + jnp.mod(position - slot_count + rotation, slab_count - 1)) % slab_count
    sorted_owner = jnp.where(position < slot_count, hot_slab, others)
    orders = jax.vmap(lambda sub_key: jax.random.permutation(sub_key, BRICK_DEV))(jax.random.split(key_order, device_count))
    owner_slab = jnp.take_along_axis(sorted_owner, orders, axis=1).reshape(BRICKS)
    offsets = jax.random.randint(key_plane, (BRICKS, ROW_ATOMS), 0, CZ)
    return (owner_slab[:, None] * CZ + offsets).astype(jnp.int32)


def draw_brick_count(key, part):
    device_count = BRICKS // BRICK_DEV
    key_base, key_full = jax.random.split(jax.random.fold_in(key, 23))
    counts = jax.random.randint(key_base, (device_count, BRICK_DEV), 32, ROW_ATOMS + 1)
    full_spot = jax.random.randint(key_full, (device_count, 1), 0, BRICK_DEV)
    position = jnp.arange(BRICK_DEV, dtype=jnp.int32)[None, :]
    counts = jnp.where(position == full_spot, ROW_ATOMS, counts)
    counts = jnp.where(position == (full_spot + 1) % BRICK_DEV, 32, counts)
    return counts.reshape(BRICKS).astype(jnp.int32)


def draw_electron_temp(key, part):
    hot_slab = hot_slab_index(key)
    key_phase, key_rough, key_cold = jax.random.split(jax.random.fold_in(key, 37), 3)
    phase = jax.random.uniform(key_phase, (1, NX, NY), jnp.float32, -math.pi, math.pi)
    depth = jnp.arange(NZ, dtype=jnp.float32)[:, None, None]
    profile = jnp.exp(0.69 * jnp.tanh(3.0 * jnp.sin(2.0 * math.pi * depth / 384.0 + phase)))
    roughness = jnp.exp(jax.random.uniform(key_rough, (NZ, NX, NY), jnp.float32, math.log(0.1), math.log(1.9)))
    cold = jax.random.uniform(key_cold, (NZ, NX, NY), jnp.float32, 0.05, 0.15)
    slab_of_plane = jnp.arange(NZ, dtype=jnp.int32)[:, None, None] // CZ
    return jnp.where(slab_of_plane == hot_slab, cold, profile * roughness).astype(jnp.float32)


def touch_ends(drawn, own_key, least, largest):
    dims = drawn.shape
    spot = [jax.random.randint(jax.random.fold_in(own_key, axis), (), 0, dims[axis]) for axis in range(len(dims))]
    drawn = drawn.at[tuple(spot)].set(least)
    longest = dims.index(max(dims))
    spot[longest] = (spot[longest] + 1) % dims[longest]
    return drawn.at[tuple(spot)].set(largest)


def block_scale(stream_key, extent, cuts, low, top_value):
    factor_of = 1.0
    for dim, blocks in cuts:
        draws = jax.random.uniform(jax.random.fold_in(jax.random.fold_in(stream_key, 6), dim), (blocks,), jnp.float32, low / len(cuts), top_value / len(cuts))
        factor_of = factor_of * jnp.repeat(jnp.exp(draws), extent[dim] // blocks).reshape((-1,) + (1,) * (len(extent) - 1 - dim))
    return factor_of


def normal_values(key, shape, deviation, limit, pieces=(), kind=jnp.bfloat16):
    loudness = block_scale(key, shape, pieces, -0.22, 0.18) if pieces else 1.0
    values = jax.random.normal(key, shape, jnp.float32) * deviation * loudness
    return jnp.minimum(jnp.maximum(values, -limit), limit).astype(kind)


def setup_inputs(seed: int = 0) -> dict:
    arg_keys = jax.random.split(jax.random.key(seed), 7)
    return {
        "atom_velocity": normal_values(arg_keys[0], (3, BRICKS, ROW_ATOMS), 0.7, 4.2, ((1, 128),), jnp.float32),
        "atom_noise": normal_values(arg_keys[1], (3, BRICKS, ROW_ATOMS), 1.0, 6.0, ((1, 128),), jnp.float32),
        "atom_plane": draw_atom_plane(jax.random.fold_in(arg_keys[6], 71), 0),
        "atom_column": touch_ends(jax.random.randint(arg_keys[3], (BRICKS, ROW_ATOMS), 0, CX * NY), jax.random.fold_in(arg_keys[3], 1), 0, (CX * NY) - 1).astype(jnp.int32),
        "brick_count": draw_brick_count(jax.random.fold_in(arg_keys[6], 71), 0),
        "electron_temp": draw_electron_temp(jax.random.fold_in(arg_keys[6], 71), 0),
    }


STIFFNESS = 10000.0
LATERAL = 0.1
COUPLE = 0.5
TWO_THIRDS = 2.0 / 3.0
KICK_RATE = 0.2

def chain_solve(lower_band, diagonal, upper_band, right_side):

    def forward(state_pair, entries):
        sweep_ratio, sweep_value = state_pair
        below_band, middle, above_band, source = entries
        pivot_value = middle - below_band * sweep_ratio
        next_ratio = above_band / pivot_value
        next_value = (source - below_band * sweep_value) / pivot_value
        return ((next_ratio, next_value), (next_ratio, next_value))
    zero_start = jnp.zeros_like(diagonal[0])
    _, (ratios, values) = lax.scan(forward, (zero_start, zero_start), (lower_band, diagonal, upper_band, right_side))

    def backward(later_value, entries):
        ratio_here, value_here = entries
        result = value_here - ratio_here * later_value
        return (result, result)
    _, solution = lax.scan(backward, zero_start, (ratios, values), reverse=True)
    return solution

def reference(atom_velocity, atom_noise, atom_plane, atom_column, brick_count, electron_temp):
    cell_total = NZ * NX * NY
    brick_ids = jnp.arange(BRICKS, dtype=jnp.int32)
    column_group = brick_ids // BRICK_DEV % N_GX
    atom_lane = jnp.arange(ROW_ATOMS, dtype=jnp.int32)
    in_use = atom_lane[None, :] < brick_count[:, None]
    x_cell = column_group[:, None] * CX + atom_column // NY
    y_cell = atom_column % NY
    atom_cell = jnp.where(in_use, (atom_plane * NX + x_cell) * NY + y_cell, cell_total).astype(jnp.int32)
    kinetic = 0.5 * lax.optimization_barrier(jnp.sum(atom_velocity * atom_velocity, axis=0))
    flat_cell = atom_cell.reshape(-1)
    energy = jax.ops.segment_sum(kinetic.reshape(-1), flat_cell, cell_total + 1)[:cell_total].reshape(NZ, NX, NY)
    atom_count = jax.ops.segment_sum(jnp.ones_like(kinetic).reshape(-1), flat_cell, cell_total + 1)[:cell_total].reshape(NZ, NX, NY)
    lateral = LATERAL * (jnp.roll(electron_temp, 1, 1) + jnp.roll(electron_temp, -1, 1) + jnp.roll(electron_temp, 1, 2) + jnp.roll(electron_temp, -1, 2) - 4.0 * electron_temp)
    face_value = STIFFNESS * (0.5 * (electron_temp[1:] + electron_temp[:-1]))
    zero_plane = jnp.zeros((1, NX, NY), jnp.float32)
    lower_face = jnp.concatenate([zero_plane, face_value], axis=0)
    upper_face = jnp.concatenate([face_value, zero_plane], axis=0)
    diagonal = electron_temp + lower_face + upper_face + COUPLE * atom_count
    right_side = electron_temp * electron_temp + lateral + COUPLE * TWO_THIRDS * energy
    new_temp = chain_solve(-lower_face, diagonal, -upper_face, right_side)
    flat_temp = jnp.concatenate([new_temp.reshape(-1), jnp.zeros((1,), jnp.float32)])
    atom_temp = flat_temp[atom_cell]
    new_velocity = jnp.where(in_use[None], (1.0 - KICK_RATE) * atom_velocity + jnp.sqrt(2.0 * KICK_RATE * atom_temp)[None] * atom_noise, 0.0)
    return (new_temp, new_velocity)
```

```python
import jax
import jax.numpy as jnp
from jax import lax
from jax.experimental import pallas as pl
from jax.experimental.pallas import tpu as pltpu
from jax.sharding import PartitionSpec as P

STIFFNESS = 10000.0
LATERAL = 0.1
COUPLE = 0.5
TWO_THIRDS = 2.0 / 3.0
KICK_RATE = 0.2
SLABS = 16
PLANES = 16
WIDTH = 16
NY = 256
SLOTS = 16
BRICKS = 128
LANES = 128
F32 = jnp.float32
BF16 = jnp.bfloat16
VMEM = pl.BlockSpec(memory_space=pltpu.VMEM)


def iota(shape, axis):
    return lax.broadcasted_iota(jnp.int32, shape, axis)


def split3(value):
    high = value.astype(BF16)
    rest = value - high.astype(F32)
    middle = rest.astype(BF16)
    low = (rest - middle.astype(F32)).astype(BF16)
    return high, middle, low


def split2(value):
    high = value.astype(BF16)
    low = (value - high.astype(F32)).astype(BF16)
    return high, low


def dot(a, b, contract=((1,), (0,))):
    return lax.dot_general(a, b, (contract, ((), ())), preferred_element_type=F32)


def used_mask(count_row):
    diagonal = iota((BRICKS, LANES), 0) == iota((BRICKS, LANES), 1)
    count_column = jnp.sum(jnp.where(diagonal, count_row.astype(F32), 0.0), axis=1, keepdims=True)
    return iota((BRICKS, LANES), 1).astype(F32) < count_column


def prep_kernel(velocity, plane, column, count, send, slot):
    used = used_mask(count[...])
    speed = velocity[...]
    kinetic = 0.5 * (speed[0] * speed[0] + speed[1] * speed[1] + speed[2] * speed[2])
    kinetic = jnp.where(used, kinetic, 0.0)
    planes = plane[...]
    columns = column[...]
    owner = planes[:, 0:1] // PLANES
    square = (BRICKS, LANES)
    hits = jnp.where(iota(square, 1) == owner, 1.0, 0.0)
    earlier = jnp.where(iota(square, 0) > iota(square, 1), 1.0, 0.0).astype(BF16)
    before = dot(earlier, hits.astype(BF16))
    rank = jnp.sum(before * hits, axis=1, keepdims=True)
    brick_slot = owner.astype(F32) * SLOTS + rank
    slot[...] = jnp.broadcast_to(brick_slot, square)
    slot_row = jnp.sum(
        jnp.where(iota(square, 0) == iota(square, 1), brick_slot, 0.0), axis=0, keepdims=True
    )
    slots = SLABS * SLOTS
    pick = jnp.where(iota((slots, BRICKS), 0).astype(F32) == slot_row, 1.0, 0.0).astype(BF16)
    row_code = (planes - owner * PLANES) * WIDTH + columns // NY + 1
    row_code = jnp.where(used, row_code, 0).astype(F32).astype(BF16)
    y_code = jnp.where(used, columns % NY, 0).astype(F32).astype(BF16)
    code = 256.0 * dot(pick, row_code) + dot(pick, y_code)
    high, middle, low = split3(kinetic)
    sent = (dot(pick, high) + dot(pick, middle)) + dot(pick, low)
    send[:, 0] = sent.reshape(SLABS, SLOTS, LANES)
    send[:, 1] = code.reshape(SLABS, SLOTS, LANES)


ROWS = PLANES * WIDTH


def bin_chunk(kinetic, code):
    whole = code.astype(jnp.int32)
    row = ((whole // 256) - 1).astype(F32)
    y = (whole % 256).astype(F32)
    high = kinetic.astype(BF16).astype(F32)
    low = kinetic - high
    row_ids = iota((ROWS, LANES), 0).astype(F32).astype(BF16)
    y_ids = row_ids
    one = jnp.ones((), BF16)
    zero = jnp.zeros((), BF16)
    left = []
    right = []
    for brick in range(SLOTS):
        at = slice(brick, brick + 1)

        def spread(value):
            return jnp.broadcast_to(value[at], (ROWS, LANES)).astype(BF16)

        hit = row_ids == spread(row)
        left.append(
            jnp.concatenate(
                [
                    jnp.where(hit, spread(high), zero),
                    jnp.where(hit, spread(low), zero),
                    jnp.where(hit, one, zero),
                ],
                axis=0,
            )
        )
        right.append(jnp.where(y_ids == spread(y), one, zero))
    return dot(
        jnp.concatenate(left, axis=1), jnp.concatenate(right, axis=1), contract=((1,), (1,))
    )


def bin_kernel(got, temp, below, left, right, reduced, fixed, to_low, to_high, totals):
    totals[...] = jnp.zeros_like(totals)

    def chunk(source, carry):
        totals[...] += bin_chunk(got[source, 0], got[source, 1])
        return carry

    lax.fori_loop(0, SLABS, chunk, 0)
    slab = lax.axis_index("gz")
    has_below = jnp.where(slab > 0, 1.0, 0.0)
    shape = (WIDTH, NY)
    lower = has_below * (STIFFNESS * (0.5 * (temp[0] + below[0])))
    ground = current = link = back_ground = back_current = None
    for p in range(PLANES):
        here = temp[p]
        rows = slice(p * WIDTH, (p + 1) * WIDTH)
        energy = totals[rows] + totals[ROWS + p * WIDTH : ROWS + (p + 1) * WIDTH]
        count = totals[2 * ROWS + p * WIDTH : 2 * ROWS + (p + 1) * WIDTH]
        x_less = jnp.concatenate([left[p], here[:-1]], axis=0)
        x_more = jnp.concatenate([here[1:], right[p]], axis=0)
        y_less = pltpu.roll(here, 1, 1)
        y_more = pltpu.roll(here, NY - 1, 1)
        lateral = LATERAL * (x_less + x_more + y_less + y_more - 4.0 * here)
        excess = here + COUPLE * count
        source = here * here + lateral + (COUPLE * TWO_THIRDS) * energy
        if p == 0:
            link, ground, current = lower, excess, source
            back_ground = back_current = jnp.zeros(shape, F32)
        else:
            upper = STIFFNESS * (0.5 * (temp[p - 1] + here))
            inverse = 1.0 / (ground + link + upper)
            high = upper * inverse
            low = link * inverse
            fixed[p - 1] = current * inverse
            to_low[p - 1] = low
            to_high[p - 1] = high
            back_ground = back_ground + low * ground
            back_current = back_current + low * current
            link = high * link
            ground = excess + high * ground
            current = source + high * current
    for place, value in enumerate([link, ground, current, back_ground, back_current]):
        reduced[:, place, :] = value


def shift_rows(value, step):
    zeros = jnp.zeros((abs(step), value.shape[1]), value.dtype)
    if step > 0:
        return jnp.concatenate([value[step:], zeros], axis=0)
    return jnp.concatenate([zeros, value[:step]], axis=0)


def reduce_kernel(got, ends):
    link, ground, current, back_ground, back_current = [got[:, place, :] for place in range(5)]
    ground = ground + shift_rows(back_ground, 1)
    current = current + shift_rows(back_current, 1)
    below = link
    above = shift_rows(link, 1)
    distance = 1
    while distance < SLABS:
        inverse = 1.0 / (ground + below + above)
        ratio_below = below * shift_rows(inverse, -distance)
        ratio_above = above * shift_rows(inverse, distance)
        ground, current, below, above = (
            ground
            + ratio_below * shift_rows(ground, -distance)
            + ratio_above * shift_rows(ground, distance),
            current
            + ratio_below * shift_rows(current, -distance)
            + ratio_above * shift_rows(current, distance),
            ratio_below * shift_rows(below, -distance),
            ratio_above * shift_rows(above, distance),
        )
        distance *= 2
    value = current / ground
    ends[:, 0, :] = shift_rows(value, -1)
    ends[:, 1, :] = value


def look_chunk(table_high, table_low, code):
    whole = code.astype(jnp.int32)
    row = ((whole // 256) - 1).astype(F32)
    y = (whole % 256).astype(F32)
    y_ids = iota((NY, LANES), 0).astype(F32).astype(BF16)
    row_ids = iota((ROWS, LANES), 0).astype(F32)
    one = jnp.ones((), BF16)
    zero = jnp.zeros((), BF16)
    right = []
    for brick in range(SLOTS):
        spread = jnp.broadcast_to(y[brick : brick + 1], (NY, LANES)).astype(BF16)
        right.append(jnp.where(y_ids == spread, one, zero))
    hot = jnp.concatenate(right, axis=1)
    picked = dot(table_high, hot) + dot(table_low, hot)
    out = []
    for brick in range(SLOTS):
        part = picked[:, brick * LANES : (brick + 1) * LANES]
        hit = row_ids == jnp.broadcast_to(row[brick : brick + 1], (ROWS, LANES))
        out.append(jnp.sum(jnp.where(hit, part, 0.0), axis=0, keepdims=True))
    return jnp.concatenate(out, axis=0)


def back_kernel(fixed, to_low, to_high, ends, got, solved, reply, high_table, low_table):
    low_end = ends[:, 0, :]
    value = ends[:, 1, :]
    for p in range(PLANES - 1, -1, -1):
        if p < PLANES - 1:
            value = (fixed[p] + to_low[p] * low_end) + to_high[p] * value
        solved[p] = value
        high, low = split2(value)
        high_table[p * WIDTH : (p + 1) * WIDTH] = high
        low_table[p * WIDTH : (p + 1) * WIDTH] = low

    def chunk(source, carry):
        reply[source] = look_chunk(high_table[...], low_table[...], got[source, 1])
        return carry

    lax.fori_loop(0, SLABS, chunk, 0)


def kick_kernel(velocity, noise, count, slot, returned, moved):
    used = used_mask(count[...])
    slots = SLABS * SLOTS
    slot_ids = iota((BRICKS, slots), 1).astype(F32)
    where_from = jnp.concatenate([slot[...], slot[...]], axis=1)
    pick = jnp.where(slot_ids == where_from, 1.0, 0.0).astype(BF16)
    high, middle, low = split3(returned[...].reshape(slots, LANES))
    temp = (dot(pick, high) + dot(pick, middle)) + dot(pick, low)
    scale = jnp.sqrt(2.0 * KICK_RATE * temp)
    for axis in range(3):
        kicked = (1.0 - KICK_RATE) * velocity[axis] + scale * noise[axis]
        moved[axis] = jnp.where(used, kicked, 0.0)


def shape(*dims):
    return jax.ShapeDtypeStruct(dims, F32)


def call(kernel, count, outs, scratch=(), **params):
    return pl.pallas_call(
        kernel,
        out_shape=outs,
        in_specs=[VMEM] * count,
        out_specs=jax.tree.map(lambda _: VMEM, outs),
        scratch_shapes=list(scratch),
        compiler_params=pltpu.CompilerParams(**params),
    )


def ring(value, axis, step, closed):
    size = lax.axis_size(axis)
    pairs = [(i, (i + step) % size) for i in range(size) if closed or 0 <= i + step < size]
    return lax.ppermute(value, axis, pairs)


def body(velocity, noise, plane, column, brick_count, temp):
    count = brick_count.reshape(1, BRICKS)
    below = ring(temp[-1:], "gz", 1, False)
    left = ring(temp[:, -1:], "gx", 1, True)
    right = ring(temp[:, :1], "gx", -1, True)
    send, slot = call(
        prep_kernel, 4, (shape(SLABS, 2, SLOTS, LANES), shape(BRICKS, LANES))
    )(velocity, plane, column, count)
    got = lax.all_to_all(send, "gz", 0, 0, tiled=True)
    inner = shape(PLANES - 1, WIDTH, NY)
    reduced, fixed, to_low, to_high = call(
        bin_kernel,
        5,
        (shape(WIDTH, 5, NY), inner, inner, inner),
        [pltpu.VMEM((3 * ROWS, NY), F32)],
    )(got, temp, below, left, right)
    systems = lax.all_to_all(reduced, "gz", 0, 0, tiled=True)
    ends = call(reduce_kernel, 1, shape(SLABS, 2, NY))(systems)
    own_ends = lax.all_to_all(ends, "gz", 0, 0, tiled=True)
    solved, reply = call(
        back_kernel,
        5,
        (shape(PLANES, WIDTH, NY), shape(SLABS, SLOTS, LANES)),
        [pltpu.VMEM((ROWS, NY), BF16)] * 2,
    )(fixed, to_low, to_high, own_ends, got)
    returned = lax.all_to_all(reply, "gz", 0, 0, tiled=True)
    moved = call(kick_kernel, 5, shape(3, BRICKS, LANES))(velocity, noise, count, slot, returned)
    return solved, moved


def solution(mesh):
    placed = (
        P(None, ("gz", "gx"), None),
        P(None, ("gz", "gx"), None),
        P(("gz", "gx"), None),
        P(("gz", "gx"), None),
        P(("gz", "gx")),
        P("gz", "gx", None),
    )
    return jax.shard_map(
        body,
        mesh=mesh,
        in_specs=placed,
        out_specs=(P("gz", "gx", None), P(None, ("gz", "gx"), None)),
        check_vma=False,
    )
```

```python
import jax
import jax.numpy as jnp
from jax import lax
from jax.experimental import pallas as pl
from jax.experimental.pallas import tpu as pltpu
from jax.sharding import PartitionSpec as P

STIFFNESS = 10000.0
LATERAL = 0.1
COUPLE = 0.5
TWO_THIRDS = 2.0 / 3.0
KICK_RATE = 0.2
SLABS = 16
PLANES = 16
WIDTH = 16
NY = 256
SLOTS = 16
BRICKS = 128
LANES = 128
F32 = jnp.float32
BF16 = jnp.bfloat16
VMEM = pl.BlockSpec(memory_space=pltpu.VMEM)


def iota(shape, axis):
    return lax.broadcasted_iota(jnp.int32, shape, axis)


def split3(value):
    high = value.astype(BF16)
    rest = value - high.astype(F32)
    middle = rest.astype(BF16)
    low = (rest - middle.astype(F32)).astype(BF16)
    return high, middle, low


def split2(value):
    high = value.astype(BF16)
    low = (value - high.astype(F32)).astype(BF16)
    return high, low


def dot(a, b, contract=((1,), (0,))):
    return lax.dot_general(a, b, (contract, ((), ())), preferred_element_type=F32)


def used_mask(count_row):
    diagonal = iota((BRICKS, LANES), 0) == iota((BRICKS, LANES), 1)
    count_column = jnp.sum(jnp.where(diagonal, count_row.astype(F32), 0.0), axis=1, keepdims=True)
    return iota((BRICKS, LANES), 1).astype(F32) < count_column


ROWS = PLANES * WIDTH


def bin_chunk(kinetic, code):
    whole = code.astype(jnp.int32)
    row = ((whole // 256) - 1).astype(F32)
    y = (whole % 256).astype(F32)
    high = kinetic.astype(BF16).astype(F32)
    low = kinetic - high
    row_ids = iota((ROWS, LANES), 0).astype(F32).astype(BF16)
    y_ids = row_ids
    one = jnp.ones((), BF16)
    zero = jnp.zeros((), BF16)
    left = []
    right = []
    for brick in range(SLOTS):
        at = slice(brick, brick + 1)

        def spread(value):
            return jnp.broadcast_to(value[at], (ROWS, LANES)).astype(BF16)

        hit = row_ids == spread(row)
        left.append(
            jnp.concatenate(
                [
                    jnp.where(hit, spread(high), zero),
                    jnp.where(hit, spread(low), zero),
                    jnp.where(hit, one, zero),
                ],
                axis=0,
            )
        )
        right.append(jnp.where(y_ids == spread(y), one, zero))
    return dot(
        jnp.concatenate(left, axis=1), jnp.concatenate(right, axis=1), contract=((1,), (1,))
    )


def shift_rows(value, step):
    zeros = jnp.zeros((abs(step), value.shape[1]), value.dtype)
    if step > 0:
        return jnp.concatenate([value[step:], zeros], axis=0)
    return jnp.concatenate([zeros, value[:step]], axis=0)


def look_chunk(table_high, table_low, code):
    whole = code.astype(jnp.int32)
    row = ((whole // 256) - 1).astype(F32)
    y = (whole % 256).astype(F32)
    y_ids = iota((NY, LANES), 0).astype(F32).astype(BF16)
    row_ids = iota((ROWS, LANES), 0).astype(F32)
    one = jnp.ones((), BF16)
    zero = jnp.zeros((), BF16)
    right = []
    for brick in range(SLOTS):
        spread = jnp.broadcast_to(y[brick : brick + 1], (NY, LANES)).astype(BF16)
        right.append(jnp.where(y_ids == spread, one, zero))
    hot = jnp.concatenate(right, axis=1)
    picked = dot(table_high, hot) + dot(table_low, hot)
    out = []
    for brick in range(SLOTS):
        part = picked[:, brick * LANES : (brick + 1) * LANES]
        hit = row_ids == jnp.broadcast_to(row[brick : brick + 1], (ROWS, LANES))
        out.append(jnp.sum(jnp.where(hit, part, 0.0), axis=0, keepdims=True))
    return jnp.concatenate(out, axis=0)


SIDE = 4
MESH = pl.DeviceIdType.MESH


def prepare(velocity, plane, column, count, send, slot, me):
    used = used_mask(count[...])
    speed = velocity[...]
    kinetic = 0.5 * (speed[0] * speed[0] + speed[1] * speed[1] + speed[2] * speed[2])
    kinetic = jnp.where(used, kinetic, 0.0)
    planes = plane[...]
    columns = column[...]
    owner = planes[:, 0:1] // PLANES
    place = (owner // SIDE - me // SIDE + SIDE) % SIDE * SIDE + (owner % SIDE - me % SIDE + SIDE) % SIDE
    square = (BRICKS, LANES)
    hits = jnp.where(iota(square, 1) == place, 1.0, 0.0)
    earlier = jnp.where(iota(square, 0) > iota(square, 1), 1.0, 0.0).astype(BF16)
    before = dot(earlier, hits.astype(BF16))
    rank = jnp.sum(before * hits, axis=1, keepdims=True)
    brick_slot = place.astype(F32) * SLOTS + rank
    slot[...] = jnp.broadcast_to(brick_slot, square)
    slot_row = jnp.sum(
        jnp.where(iota(square, 0) == iota(square, 1), brick_slot, 0.0), axis=0, keepdims=True
    )
    slots = SLABS * SLOTS
    pick = jnp.where(iota((slots, BRICKS), 0).astype(F32) == slot_row, 1.0, 0.0).astype(BF16)
    row_code = (planes - owner * PLANES) * WIDTH + columns // NY + 1
    row_code = jnp.where(used, row_code, 0).astype(F32).astype(BF16)
    y_code = jnp.where(used, columns % NY, 0).astype(F32).astype(BF16)
    code = 256.0 * dot(pick, row_code) + dot(pick, y_code)
    high, middle, low = split3(kinetic)
    sent = (dot(pick, high) + dot(pick, middle)) + dot(pick, low)
    send[:, 0] = sent.reshape(SLABS, SLOTS, LANES)
    send[:, 1] = code.reshape(SLABS, SLOTS, LANES)


def eliminate(temp, below, left, right, slab, totals, reduced, fixed, to_low, to_high):
    has_below = jnp.where(slab > 0, 1.0, 0.0)
    shape = (WIDTH, NY)
    lower = has_below * (STIFFNESS * (0.5 * (temp[0] + below[...])))
    ground = current = link = back_ground = back_current = None
    for p in range(PLANES):
        here = temp[p]
        energy = totals[p * WIDTH : (p + 1) * WIDTH] + totals[ROWS + p * WIDTH : ROWS + (p + 1) * WIDTH]
        count = totals[2 * ROWS + p * WIDTH : 2 * ROWS + (p + 1) * WIDTH]
        x_less = jnp.concatenate([left[p : p + 1], here[:-1]], axis=0)
        x_more = jnp.concatenate([here[1:], right[p : p + 1]], axis=0)
        y_less = pltpu.roll(here, 1, 1)
        y_more = pltpu.roll(here, NY - 1, 1)
        lateral = LATERAL * (x_less + x_more + y_less + y_more - 4.0 * here)
        excess = here + COUPLE * count
        source = here * here + lateral + (COUPLE * TWO_THIRDS) * energy
        if p == 0:
            link, ground, current = lower, excess, source
            back_ground = back_current = jnp.zeros(shape, F32)
        else:
            upper = STIFFNESS * (0.5 * (temp[p - 1] + here))
            inverse = 1.0 / (ground + link + upper)
            high = upper * inverse
            low = link * inverse
            fixed[p - 1] = current * inverse
            to_low[p - 1] = low
            to_high[p - 1] = high
            back_ground = back_ground + low * ground
            back_current = back_current + low * current
            link = high * link
            ground = excess + high * ground
            current = source + high * current
    for place, value in enumerate([link, ground, current, back_ground, back_current]):
        reduced[:, place, :] = value


def solve_reduced(systems, ends):
    link, ground, current, back_ground, back_current = [systems[:, place, :] for place in range(5)]
    ground = ground + shift_rows(back_ground, 1)
    current = current + shift_rows(back_current, 1)
    below = link
    above = shift_rows(link, 1)
    distance = 1
    while distance < SLABS:
        inverse = 1.0 / (ground + below + above)
        ratio_below = below * shift_rows(inverse, -distance)
        ratio_above = above * shift_rows(inverse, distance)
        ground, current, below, above = (
            ground
            + ratio_below * shift_rows(ground, -distance)
            + ratio_above * shift_rows(ground, distance),
            current
            + ratio_below * shift_rows(current, -distance)
            + ratio_above * shift_rows(current, distance),
            ratio_below * shift_rows(below, -distance),
            ratio_above * shift_rows(above, distance),
        )
        distance *= 2
    value = current / ground
    ends[:, 0, :] = shift_rows(value, -1)
    ends[:, 1, :] = value


def substitute(fixed, to_low, to_high, ends, solved, high_table, low_table):
    low_end = ends[:, 0, :]
    value = ends[:, 1, :]
    for p in range(PLANES - 1, -1, -1):
        if p < PLANES - 1:
            value = (fixed[p] + to_low[p] * low_end) + to_high[p] * value
        solved[p] = value
        high, low = split2(value)
        high_table[p * WIDTH : (p + 1) * WIDTH] = high
        low_table[p * WIDTH : (p + 1) * WIDTH] = low


def kick(velocity, noise, count, slot, returned, moved):
    used = used_mask(count[...])
    slots = SLABS * SLOTS
    slot_ids = iota((BRICKS, slots), 1).astype(F32)
    where_from = jnp.concatenate([slot[...], slot[...]], axis=1)
    pick = jnp.where(slot_ids == where_from, 1.0, 0.0).astype(BF16)
    high, middle, low = split3(returned[...].reshape(slots, LANES))
    temp = (dot(pick, high) + dot(pick, middle)) + dot(pick, low)
    scale = jnp.sqrt(2.0 * KICK_RATE * temp)
    for axis in range(3):
        kicked = (1.0 - KICK_RATE) * velocity[axis] + scale * noise[axis]
        moved[axis] = jnp.where(used, kicked, 0.0)


def step_kernel(
    velocity_in, noise_in, plane_in, column_in, count_in, temp_in,
    solved_out, moved_out,
    velocity, noise, plane, column, count, temp,
    send, got, slot, edges, below, sides, totals, reduced, systems, ends, own_ends,
    fixed, to_low, to_high, solved, high_table, low_table, reply, returned, moved,
    load_sem, store_sem, halo_send, halo_recv,
    atom_send, atom_recv, system_send, system_recv, end_send, end_recv, reply_send, reply_recv,
):
    me = lax.axis_index("gz")
    line = lax.axis_index("gx")
    lines = lax.axis_size("gx")
    next_line = lax.rem(line + 1, lines)
    last_line = lax.rem(line + lines - 1, lines)
    deep, wide = me // SIDE, me % SIDE

    def ahead(place):
        return (deep + place // SIDE) % SIDE * SIDE + (wide + place % SIDE) % SIDE

    def behind(place):
        return (deep + SIDE - place // SIDE) % SIDE * SIDE + (wide + SIDE - place % SIDE) % SIDE

    def remote(source, target, sent, received, where):
        return pltpu.make_async_remote_copy(
            src_ref=source, dst_ref=target, send_sem=sent, recv_sem=received,
            device_id=where, device_id_type=MESH,
        )

    loads = [
        pltpu.make_async_copy(source, target, load_sem.at[place])
        for place, (source, target) in enumerate(
            [
                (plane_in, plane),
                (column_in, column),
                (count_in, count),
                (velocity_in, velocity),
                (temp_in, temp),
                (noise_in, noise),
            ]
        )
    ]
    for load in loads:
        load.start()
    barrier = pltpu.get_barrier_semaphore()
    for place in range(1, SLABS):
        pl.semaphore_signal(barrier, inc=1, device_id={"gz": ahead(place)}, device_id_type=MESH)
    for where in (next_line, last_line):
        pl.semaphore_signal(barrier, inc=1, device_id={"gx": where}, device_id_type=MESH)
    for load in loads[:4]:
        load.wait()
    prepare(velocity, plane, column, count, send, slot, me)
    pl.semaphore_wait(barrier, SLABS + 1)

    def atoms(place):
        return remote(
            send.at[place], got.at[place], atom_send.at[place], atom_recv.at[place], {"gz": ahead(place)}
        )

    for place in range(1, SLABS):
        atoms(place).start()
    got[0] = send[0]
    loads[4].wait()
    edges[0] = temp[:, 0, :]
    edges[1] = temp[:, WIDTH - 1, :]
    halos = [
        remote(temp.at[PLANES - 1], below, halo_send.at[0], halo_recv.at[0], {"gz": (me + 1) % SLABS}),
        remote(edges.at[1], sides.at[0], halo_send.at[1], halo_recv.at[1], {"gx": next_line}),
        remote(edges.at[0], sides.at[1], halo_send.at[2], halo_recv.at[2], {"gx": last_line}),
    ]
    for halo in halos:
        halo.start()

    totals[...] = jnp.zeros_like(totals)

    def add_chunk(place, carry):
        @pl.when(place > 0)
        def _():
            atoms(place).wait_recv()

        totals[...] += bin_chunk(got[place, 0], got[place, 1])
        return carry

    lax.fori_loop(0, SLABS, add_chunk, 0)
    for halo in halos:
        halo.wait_recv()
    eliminate(temp, below, sides.at[0], sides.at[1], me, totals, reduced, fixed, to_low, to_high)

    def system(place):
        return remote(
            reduced.at[ahead(place)], systems.at[me], system_send.at[place], system_recv.at[place],
            {"gz": ahead(place)},
        )

    for place in range(1, SLABS):
        system(place).start()
    systems[me] = reduced[me]
    for place in range(1, SLABS):
        system(place).wait_recv()
    solve_reduced(systems, ends)

    def end(place):
        return remote(
            ends.at[ahead(place)], own_ends.at[me], end_send.at[place], end_recv.at[place],
            {"gz": ahead(place)},
        )

    for place in range(1, SLABS):
        end(place).start()
    own_ends[me] = ends[me]
    for place in range(1, SLABS):
        end(place).wait_recv()
    substitute(fixed, to_low, to_high, own_ends, solved, high_table, low_table)
    keep = pltpu.make_async_copy(solved, solved_out, store_sem.at[0])
    keep.start()

    def answer(place):
        return remote(
            reply.at[place], returned.at[place], reply_send.at[place], reply_recv.at[place],
            {"gz": behind(place)},
        )

    def look(turn, carry):
        place = SLABS - 1 - turn
        reply[place] = look_chunk(high_table[...], low_table[...], got[place, 1])

        @pl.when(place > 0)
        def _():
            answer(place).start()

        return carry

    lax.fori_loop(0, SLABS, look, 0)
    returned[0] = reply[0]
    loads[5].wait()
    for place in range(1, SLABS):
        answer(place).wait_recv()
    kick(velocity, noise, count, slot, returned, moved)
    leave = pltpu.make_async_copy(moved, moved_out, store_sem.at[1])
    leave.start()
    for halo in halos:
        halo.wait_send()
    for place in range(1, SLABS):
        atoms(place).wait_send()
        system(place).wait_send()
        end(place).wait_send()
        answer(place).wait_send()
    keep.wait()
    leave.wait()


def shape(*dims):
    return jax.ShapeDtypeStruct(dims, F32)


def body(velocity, noise, plane, column, brick_count, temp):
    count = brick_count.reshape(1, BRICKS)
    vmem = pltpu.VMEM
    inner = vmem((PLANES - 1, WIDTH, NY), F32)
    chunk = vmem((SLABS, 2, SLOTS, LANES), F32)
    line = vmem((SLABS, SLOTS, LANES), F32)
    table = vmem((ROWS, NY), BF16)
    pairs = pltpu.SemaphoreType.DMA((SLABS,))
    return pl.pallas_call(
        step_kernel,
        out_shape=(shape(PLANES, WIDTH, NY), shape(3, BRICKS, LANES)),
        in_specs=[pl.BlockSpec(memory_space=pl.ANY)] * 6,
        out_specs=(pl.BlockSpec(memory_space=pl.ANY),) * 2,
        scratch_shapes=[
            vmem((3, BRICKS, LANES), F32),
            vmem((3, BRICKS, LANES), F32),
            vmem((BRICKS, LANES), jnp.int32),
            vmem((BRICKS, LANES), jnp.int32),
            vmem((1, BRICKS), jnp.int32),
            vmem((PLANES, WIDTH, NY), F32),
            chunk,
            chunk,
            vmem((BRICKS, LANES), F32),
            vmem((2, PLANES, NY), F32),
            vmem((WIDTH, NY), F32),
            vmem((2, PLANES, NY), F32),
            vmem((3 * ROWS, NY), F32),
            vmem((WIDTH, 5, NY), F32),
            vmem((SLABS, 5, NY), F32),
            vmem((SLABS, 2, NY), F32),
            vmem((WIDTH, 2, NY), F32),
            inner,
            inner,
            inner,
            vmem((PLANES, WIDTH, NY), F32),
            table,
            table,
            line,
            line,
            vmem((3, BRICKS, LANES), F32),
            pltpu.SemaphoreType.DMA((6,)),
            pltpu.SemaphoreType.DMA((2,)),
            pltpu.SemaphoreType.DMA((3,)),
            pltpu.SemaphoreType.DMA((3,)),
        ]
        + [pairs] * 8,
        compiler_params=pltpu.CompilerParams(collective_id=0, has_side_effects=True),
    )(velocity, noise, plane, column, count, temp)


def solution(mesh):
    placed = (
        P(None, ("gz", "gx"), None),
        P(None, ("gz", "gx"), None),
        P(("gz", "gx"), None),
        P(("gz", "gx"), None),
        P(("gz", "gx")),
        P("gz", "gx", None),
    )
    return jax.shard_map(
        body,
        mesh=mesh,
        in_specs=placed,
        out_specs=(P("gz", "gx", None), P(None, ("gz", "gx"), None)),
        check_vma=False,
    )
```

```python
import jax
import jax.numpy as jnp
from jax import lax
from jax.experimental import pallas as pl
from jax.experimental.pallas import tpu as pltpu
from jax.sharding import PartitionSpec as P

STIFFNESS = 10000.0
LATERAL = 0.1
COUPLE = 0.5
TWO_THIRDS = 2.0 / 3.0
KICK_RATE = 0.2
SLABS = 16
PLANES = 16
WIDTH = 16
NY = 256
SLOTS = 16
BRICKS = 128
LANES = 128
F32 = jnp.float32
BF16 = jnp.bfloat16
VMEM = pl.BlockSpec(memory_space=pltpu.VMEM)


def iota(shape, axis):
    return lax.broadcasted_iota(jnp.int32, shape, axis)


def split3(value):
    high = value.astype(BF16)
    rest = value - high.astype(F32)
    middle = rest.astype(BF16)
    low = (rest - middle.astype(F32)).astype(BF16)
    return high, middle, low


def split2(value):
    high = value.astype(BF16)
    low = (value - high.astype(F32)).astype(BF16)
    return high, low


def dot(a, b, contract=((1,), (0,))):
    return lax.dot_general(a, b, (contract, ((), ())), preferred_element_type=F32)


def used_mask(count_row):
    diagonal = iota((BRICKS, LANES), 0) == iota((BRICKS, LANES), 1)
    count_column = jnp.sum(jnp.where(diagonal, count_row.astype(F32), 0.0), axis=1, keepdims=True)
    return iota((BRICKS, LANES), 1).astype(F32) < count_column


ROWS = PLANES * WIDTH


HALF = ROWS // 2
LOW_WEIGHT, HIGH_WEIGHT = 1.0 / 16.0, 256.0


def decode(code):
    whole = code.astype(jnp.int32)
    return whole // 256 - 1, whole % 256


def constant(value):
    return jnp.full((), value, BF16)


def bin_chunk(kinetic, code):
    row, y = decode(code)
    row, y = row.astype(F32), y.astype(F32)
    high = kinetic.astype(BF16).astype(F32)
    low = kinetic - high
    ids = iota((ROWS, LANES), 0).astype(F32).astype(BF16)
    zero = constant(0.0)
    left = []
    right = []
    for brick in range(SLOTS):

        def spread(value):
            return jnp.broadcast_to(value[brick : brick + 1], (ROWS, LANES)).astype(BF16)

        hit = ids == spread(row)
        second = jnp.where(hit[HALF:], constant(HIGH_WEIGHT), zero)
        left.append(
            jnp.concatenate(
                [
                    jnp.where(hit, spread(high), zero),
                    jnp.where(hit, spread(low), zero),
                    jnp.where(hit[:HALF], constant(LOW_WEIGHT), second),
                ],
                axis=0,
            )
        )
        right.append(jnp.where(ids == spread(y), constant(1.0), zero))
    return dot(
        jnp.concatenate(left, axis=1), jnp.concatenate(right, axis=1), contract=((1,), (1,))
    )


def add_up(values):
    while len(values) > 1:
        values = [sum(values[i : i + 2]) for i in range(0, len(values), 2)]
    return values[0]


def bin_group(chunks, energy, counts, first):
    parts = [bin_chunk(kinetic, code) for kinetic, code in chunks]
    packed = [part[2 * ROWS :] for part in parts]
    upper = [jnp.floor(part * (1.0 / HIGH_WEIGHT)) for part in packed]
    lower = [part - HIGH_WEIGHT * more for part, more in zip(packed, upper)]
    sums = [
        add_up([part[:ROWS] + part[ROWS : 2 * ROWS] for part in parts]),
        add_up(lower) * (1.0 / LOW_WEIGHT),
        add_up(upper),
    ]
    places = [(energy, slice(None)), (counts, slice(0, HALF)), (counts, slice(HALF, ROWS))]
    for (target, rows), value in zip(places, sums):
        target[rows] = value if first else target[rows] + value


def shift_rows(value, step):
    zeros = jnp.zeros((abs(step), value.shape[1]), value.dtype)
    if step > 0:
        return jnp.concatenate([value[step:], zeros], axis=0)
    return jnp.concatenate([zeros, value[:step]], axis=0)


def look_chunk(high_table, low_table, code):
    row, y = decode(code)
    row, y = row.astype(F32), y.astype(F32)
    y_ids = iota((NY, LANES), 0).astype(F32).astype(BF16)
    row_ids = iota((ROWS, LANES), 0).astype(F32)
    right = []
    for brick in range(SLOTS):
        spread = jnp.broadcast_to(y[brick : brick + 1], (NY, LANES)).astype(BF16)
        right.append(jnp.where(y_ids == spread, constant(1.0), constant(0.0)))
    hot = jnp.concatenate(right, axis=1)
    picked = dot(high_table, hot) + dot(low_table, hot)
    out = []
    for brick in range(SLOTS):
        part = picked[:, brick * LANES : (brick + 1) * LANES]
        hit = row_ids == jnp.broadcast_to(row[brick : brick + 1], (ROWS, LANES))
        out.append(jnp.sum(jnp.where(hit, part, 0.0), axis=0, keepdims=True))
    return jnp.concatenate(out, axis=0)


SIDE = 4
MESH = pl.DeviceIdType.MESH


def prepare(velocity, plane, column, count, send, slot, me):
    used = used_mask(count[...])
    speed = velocity[...]
    kinetic = 0.5 * (speed[0] * speed[0] + speed[1] * speed[1] + speed[2] * speed[2])
    kinetic = jnp.where(used, kinetic, 0.0)
    planes = plane[...]
    columns = column[...]
    owner = planes[:, 0:1] // PLANES
    place = (owner // SIDE - me // SIDE + SIDE) % SIDE * SIDE + (owner % SIDE - me % SIDE + SIDE) % SIDE
    square = (BRICKS, LANES)
    hits = jnp.where(iota(square, 1) == place, 1.0, 0.0)
    earlier = jnp.where(iota(square, 0) > iota(square, 1), 1.0, 0.0).astype(BF16)
    before = dot(earlier, hits.astype(BF16))
    rank = jnp.sum(before * hits, axis=1, keepdims=True)
    brick_slot = place.astype(F32) * SLOTS + rank
    slot[...] = jnp.broadcast_to(brick_slot, square)
    slot_row = jnp.sum(
        jnp.where(iota(square, 0) == iota(square, 1), brick_slot, 0.0), axis=0, keepdims=True
    )
    slots = SLABS * SLOTS
    pick = jnp.where(iota((slots, BRICKS), 0).astype(F32) == slot_row, 1.0, 0.0).astype(BF16)
    row_code = (planes - owner * PLANES) * WIDTH + columns // NY + 1
    row_code = jnp.where(used, row_code, 0).astype(F32).astype(BF16)
    y_code = jnp.where(used, columns % NY, 0).astype(F32).astype(BF16)
    code = 256.0 * dot(pick, row_code) + dot(pick, y_code)
    high, middle, low = split3(kinetic)
    sent = (dot(pick, high) + dot(pick, middle)) + dot(pick, low)
    send[:, 0] = sent.reshape(SLABS, SLOTS, LANES)
    send[:, 1] = code.reshape(SLABS, SLOTS, LANES)


def eliminate(temp, below, left, right, slab, energies, counts, reduced, fixed, to_low, to_high):
    has_below = jnp.where(slab > 0, 1.0, 0.0)
    shape = (WIDTH, NY)
    lower = has_below * (STIFFNESS * (0.5 * (temp[0] + below[...])))
    ground = current = link = back_ground = back_current = None
    for p in range(PLANES):
        here = temp[p]
        energy = energies[p * WIDTH : (p + 1) * WIDTH]
        count = counts[p * WIDTH : (p + 1) * WIDTH]
        x_less = jnp.concatenate([left[p : p + 1], here[:-1]], axis=0)
        x_more = jnp.concatenate([here[1:], right[p : p + 1]], axis=0)
        y_less = pltpu.roll(here, 1, 1)
        y_more = pltpu.roll(here, NY - 1, 1)
        lateral = LATERAL * (x_less + x_more + y_less + y_more - 4.0 * here)
        excess = here + COUPLE * count
        source = here * here + lateral + (COUPLE * TWO_THIRDS) * energy
        if p == 0:
            link, ground, current = lower, excess, source
            back_ground = back_current = jnp.zeros(shape, F32)
        else:
            upper = STIFFNESS * (0.5 * (temp[p - 1] + here))
            inverse = 1.0 / (ground + link + upper)
            high = upper * inverse
            low = link * inverse
            fixed[p - 1] = current * inverse
            to_low[p - 1] = low
            to_high[p - 1] = high
            back_ground = back_ground + low * ground
            back_current = back_current + low * current
            link = high * link
            ground = excess + high * ground
            current = source + high * current
    for place, value in enumerate([link, ground, current, back_ground, back_current]):
        reduced[:, place, :] = value


def solve_reduced(systems, ends):
    link, ground, current, back_ground, back_current = [systems[:, place, :] for place in range(5)]
    ground = ground + shift_rows(back_ground, 1)
    current = current + shift_rows(back_current, 1)
    below = link
    above = shift_rows(link, 1)
    distance = 1
    while distance < SLABS:
        inverse = 1.0 / (ground + below + above)
        ratio_below = below * shift_rows(inverse, -distance)
        ratio_above = above * shift_rows(inverse, distance)
        ground, current, below, above = (
            ground
            + ratio_below * shift_rows(ground, -distance)
            + ratio_above * shift_rows(ground, distance),
            current
            + ratio_below * shift_rows(current, -distance)
            + ratio_above * shift_rows(current, distance),
            ratio_below * shift_rows(below, -distance),
            ratio_above * shift_rows(above, distance),
        )
        distance *= 2
    value = current / ground
    ends[:, 0, :] = shift_rows(value, -1)
    ends[:, 1, :] = value


def substitute(fixed, to_low, to_high, ends, solved, high_table, low_table):
    low_end = ends[:, 0, :]
    value = ends[:, 1, :]
    for p in range(PLANES - 1, -1, -1):
        if p < PLANES - 1:
            value = (fixed[p] + to_low[p] * low_end) + to_high[p] * value
        solved[p] = value
        high, low = split2(value)
        high_table[p * WIDTH : (p + 1) * WIDTH] = high
        low_table[p * WIDTH : (p + 1) * WIDTH] = low


def kick(velocity, noise, count, slot, returned, moved):
    used = used_mask(count[...])
    slots = SLABS * SLOTS
    slot_ids = iota((BRICKS, slots), 1).astype(F32)
    where_from = jnp.concatenate([slot[...], slot[...]], axis=1)
    pick = jnp.where(slot_ids == where_from, 1.0, 0.0).astype(BF16)
    high, middle, low = split3(returned[...].reshape(slots, LANES))
    temp = (dot(pick, high) + dot(pick, middle)) + dot(pick, low)
    scale = jnp.sqrt(2.0 * KICK_RATE * temp)
    for axis in range(3):
        kicked = (1.0 - KICK_RATE) * velocity[axis] + scale * noise[axis]
        moved[axis] = jnp.where(used, kicked, 0.0)


def step_kernel(
    velocity_in, noise_in, plane_in, column_in, count_in, temp_in,
    solved, moved,
    velocity, noise, plane, column, count, temp,
    send, got, slot, edges, below, sides, energies, counts, reduced, systems, ends, own_ends,
    fixed, to_low, to_high, high_table, low_table, reply, returned,
    load_sem, halo_send, halo_recv,
    atom_send, atom_recv, system_send, system_recv, end_send, end_recv, reply_send, reply_recv,
):
    me = lax.axis_index("gz")
    line = lax.axis_index("gx")
    lines = lax.axis_size("gx")
    next_line = lax.rem(line + 1, lines)
    last_line = lax.rem(line + lines - 1, lines)
    deep, wide = me // SIDE, me % SIDE

    def ahead(place):
        return (deep + place // SIDE) % SIDE * SIDE + (wide + place % SIDE) % SIDE

    def behind(place):
        return (deep + SIDE - place // SIDE) % SIDE * SIDE + (wide + SIDE - place % SIDE) % SIDE

    def remote(source, target, sent, received, where):
        return pltpu.make_async_remote_copy(
            src_ref=source, dst_ref=target, send_sem=sent, recv_sem=received,
            device_id=where, device_id_type=MESH,
        )

    loads = [
        pltpu.make_async_copy(source, target, load_sem.at[place])
        for place, (source, target) in enumerate(
            [
                (plane_in, plane),
                (column_in, column),
                (count_in, count),
                (velocity_in, velocity),
                (temp_in, temp),
                (noise_in, noise),
            ]
        )
    ]
    for load in loads:
        load.start()
    barrier = pltpu.get_barrier_semaphore()
    for place in range(1, SLABS):
        pl.semaphore_signal(barrier, inc=1, device_id={"gz": ahead(place)}, device_id_type=MESH)
    for where in (next_line, last_line):
        pl.semaphore_signal(barrier, inc=1, device_id={"gx": where}, device_id_type=MESH)
    for load in loads[:4]:
        load.wait()
    prepare(velocity, plane, column, count, send, slot, me)
    bin_group([(send[0, 0], send[0, 1])], energies, counts, True)
    pl.semaphore_wait(barrier, SLABS + 1)

    def atoms(place):
        return remote(
            send.at[place], got.at[place], atom_send.at[place], atom_recv.at[place], {"gz": ahead(place)}
        )

    for place in range(1, SLABS):
        atoms(place).start()
    loads[4].wait()
    edges[0] = temp[:, 0, :]
    edges[1] = temp[:, WIDTH - 1, :]
    halos = [
        remote(temp.at[PLANES - 1], below, halo_send.at[0], halo_recv.at[0], {"gz": (me + 1) % SLABS}),
        remote(edges.at[1], sides.at[0], halo_send.at[1], halo_recv.at[1], {"gx": next_line}),
        remote(edges.at[0], sides.at[1], halo_send.at[2], halo_recv.at[2], {"gx": last_line}),
    ]
    for halo in halos:
        halo.start()

    def bin_places(places):
        for place in places:
            atoms(place).wait_recv()
        bin_group([(got[place, 0], got[place, 1]) for place in places], energies, counts, False)

    bin_places(range(1, SIDE))

    def bin_turn(turn, carry):
        bin_places([turn * SIDE + i for i in range(SIDE)])
        return carry

    lax.fori_loop(1, SIDE, bin_turn, 0)
    for halo in halos:
        halo.wait_recv()
    eliminate(temp, below, sides.at[0], sides.at[1], me, energies, counts, reduced, fixed, to_low, to_high)

    def system(place):
        return remote(
            reduced.at[ahead(place)], systems.at[me], system_send.at[place], system_recv.at[place],
            {"gz": ahead(place)},
        )

    for place in range(1, SLABS):
        system(place).start()
    systems[me] = reduced[me]
    for place in range(1, SLABS):
        system(place).wait_recv()
    solve_reduced(systems, ends)

    def end(place):
        return remote(
            ends.at[ahead(place)], own_ends.at[me], end_send.at[place], end_recv.at[place],
            {"gz": ahead(place)},
        )

    for place in range(1, SLABS):
        end(place).start()
    own_ends[me] = ends[me]
    for place in range(1, SLABS):
        end(place).wait_recv()
    substitute(fixed, to_low, to_high, own_ends, solved, high_table, low_table)

    def answer(place):
        return remote(
            reply.at[place], returned.at[place], reply_send.at[place], reply_recv.at[place],
            {"gz": behind(place)},
        )

    def look_places(places, target):
        values = [
            look_chunk(high_table[...], low_table[...], source[place, 1]) for source, place in places
        ]
        for (_, place), value in zip(places, values):
            target[place] = value

    def look_turn(turn, carry):
        places = [(SIDE - 1 - turn) * SIDE + i for i in range(SIDE)]
        look_places([(got, place) for place in places], reply)
        for place in places:
            answer(place).start()
        return carry

    lax.fori_loop(0, SIDE - 1, look_turn, 0)
    look_places([(got, place) for place in range(1, SIDE)], reply)
    for place in range(1, SIDE):
        answer(place).start()
    look_places([(send, 0)], returned)
    loads[5].wait()
    for place in range(1, SLABS):
        answer(place).wait_recv()
    kick(velocity, noise, count, slot, returned, moved)
    for halo in halos:
        halo.wait_send()
    for place in range(1, SLABS):
        atoms(place).wait_send()
        system(place).wait_send()
        end(place).wait_send()
        answer(place).wait_send()


def store_kernel(solved, moved, solved_out, moved_out, sems):
    copies = [
        pltpu.make_async_copy(solved, solved_out, sems.at[0]),
        pltpu.make_async_copy(moved, moved_out, sems.at[1]),
    ]
    for copy in copies:
        copy.start()
    for copy in copies:
        copy.wait()


def shape(*dims):
    return jax.ShapeDtypeStruct(dims, F32)


def body(velocity, noise, plane, column, brick_count, temp):
    count = brick_count.reshape(1, BRICKS)
    vmem = pltpu.VMEM
    inner = vmem((PLANES - 1, WIDTH, NY), F32)
    chunk = vmem((SLABS, 2, SLOTS, LANES), F32)
    line = vmem((SLABS, SLOTS, LANES), F32)
    table = vmem((ROWS, NY), BF16)
    pairs = pltpu.SemaphoreType.DMA((SLABS,))
    outs = (shape(PLANES, WIDTH, NY), shape(3, BRICKS, LANES))
    solved, moved = pl.pallas_call(
        step_kernel,
        out_shape=(vmem((PLANES, WIDTH, NY), F32), vmem((3, BRICKS, LANES), F32)),
        in_specs=[pl.BlockSpec(memory_space=pl.ANY)] * 6,
        out_specs=(pl.BlockSpec(memory_space=pltpu.VMEM),) * 2,
        scratch_shapes=[
            vmem((3, BRICKS, LANES), F32),
            vmem((3, BRICKS, LANES), F32),
            vmem((BRICKS, LANES), jnp.int32),
            vmem((BRICKS, LANES), jnp.int32),
            vmem((1, BRICKS), jnp.int32),
            vmem((PLANES, WIDTH, NY), F32),
            chunk,
            chunk,
            vmem((BRICKS, LANES), F32),
            vmem((2, PLANES, NY), F32),
            vmem((WIDTH, NY), F32),
            vmem((2, PLANES, NY), F32),
            vmem((ROWS, NY), F32),
            vmem((ROWS, NY), F32),
            vmem((WIDTH, 5, NY), F32),
            vmem((SLABS, 5, NY), F32),
            vmem((SLABS, 2, NY), F32),
            vmem((WIDTH, 2, NY), F32),
            inner,
            inner,
            inner,
            table,
            table,
            line,
            line,
            pltpu.SemaphoreType.DMA((6,)),
            pltpu.SemaphoreType.DMA((3,)),
            pltpu.SemaphoreType.DMA((3,)),
        ]
        + [pairs] * 8,
        compiler_params=pltpu.CompilerParams(collective_id=0, has_side_effects=True),
    )(velocity, noise, plane, column, count, temp)
    return pl.pallas_call(
        store_kernel,
        out_shape=outs,
        in_specs=[pl.BlockSpec(memory_space=pltpu.VMEM)] * 2,
        out_specs=(pl.BlockSpec(memory_space=pl.ANY),) * 2,
        scratch_shapes=[pltpu.SemaphoreType.DMA((2,))],
    )(*[pltpu.with_memory_space_constraint(value, pltpu.VMEM) for value in (solved, moved)])


def solution(mesh):
    placed = (
        P(None, ("gz", "gx"), None),
        P(None, ("gz", "gx"), None),
        P(("gz", "gx"), None),
        P(("gz", "gx"), None),
        P(("gz", "gx")),
        P("gz", "gx", None),
    )
    return jax.shard_map(
        body,
        mesh=mesh,
        in_specs=placed,
        out_specs=(P("gz", "gx", None), P(None, ("gz", "gx"), None)),
        check_vma=False,
    )
```

```python
import jax
import jax.numpy as jnp
from jax import lax
from jax.experimental import pallas as pl
from jax.experimental.pallas import tpu as pltpu
from jax.sharding import PartitionSpec as P

STIFFNESS = 10000.0
LATERAL = 0.1
COUPLE = 0.5
TWO_THIRDS = 2.0 / 3.0
KICK_RATE = 0.2
SLABS = 16
PLANES = 16
WIDTH = 16
NY = 256
SLOTS = 16
BRICKS = 128
LANES = 128
F32 = jnp.float32
BF16 = jnp.bfloat16
VMEM = pl.BlockSpec(memory_space=pltpu.VMEM)


def iota(shape, axis):
    return lax.broadcasted_iota(jnp.int32, shape, axis)


def split3(value):
    high = value.astype(BF16)
    rest = value - high.astype(F32)
    middle = rest.astype(BF16)
    low = (rest - middle.astype(F32)).astype(BF16)
    return high, middle, low


def split2(value):
    high = value.astype(BF16)
    low = (value - high.astype(F32)).astype(BF16)
    return high, low


def dot(a, b, contract=((1,), (0,))):
    return lax.dot_general(a, b, (contract, ((), ())), preferred_element_type=F32)


def used_mask(count_row):
    diagonal = iota((BRICKS, LANES), 0) == iota((BRICKS, LANES), 1)
    count_column = jnp.sum(jnp.where(diagonal, count_row.astype(F32), 0.0), axis=1, keepdims=True)
    return iota((BRICKS, LANES), 1).astype(F32) < count_column


ROWS = PLANES * WIDTH


F8 = jnp.float8_e4m3fn
LOW_SCALE = 4096.0


def decode(code):
    whole = code.astype(jnp.int32)
    return whole // 256 - 1, whole % 256


def constant(value):
    return jnp.full((), value, BF16)


def bin_chunk(kinetic, code):
    row, y = decode(code)
    row, y = row.astype(F32), y.astype(F32)
    high = kinetic.astype(BF16).astype(F32)
    low = (kinetic - high) * LOW_SCALE
    ids = iota((ROWS, LANES), 0).astype(F32).astype(BF16)
    one, zero = constant(1.0), constant(0.0)
    left, left_low, right = [], [], []
    for brick in range(SLOTS):

        def spread(value):
            return jnp.broadcast_to(value[brick : brick + 1], (ROWS, LANES)).astype(BF16)

        hit = ids == spread(row)
        left.append(jnp.where(hit, spread(high), zero))
        left_low.append(
            jnp.concatenate(
                [
                    jnp.where(hit, spread(low), zero).astype(F8),
                    jnp.where(hit, one, zero).astype(F8),
                ],
                axis=0,
            )
        )
        right.append(jnp.where(ids == spread(y), one, zero))
    last = ((1,), (1,))
    upper = dot(jnp.concatenate(left, axis=1), jnp.concatenate(right, axis=1), contract=last)
    right_low = jnp.concatenate([value.astype(F8) for value in right], axis=1)
    rest = dot(jnp.concatenate(left_low, axis=1), right_low, contract=last)
    return upper + rest[:ROWS] * (1.0 / LOW_SCALE), rest[ROWS:]


def add_up(values):
    while len(values) > 1:
        values = [sum(values[i : i + 2]) for i in range(0, len(values), 2)]
    return values[0]


def bin_group(chunks, energy, counts, first):
    parts = [bin_chunk(kinetic, code) for kinetic, code in chunks]
    for target, values in zip((energy, counts), zip(*parts)):
        value = add_up(list(values))
        target[...] = value if first else target[...] + value


def shift_rows(value, step):
    zeros = jnp.zeros((abs(step), value.shape[1]), value.dtype)
    if step > 0:
        return jnp.concatenate([value[step:], zeros], axis=0)
    return jnp.concatenate([zeros, value[:step]], axis=0)


BAND = 8


def bit_of(value, bit):
    return ((value >> bit) & 1) == 1


def look_product(high_table, low_table, code):
    row, y = decode(code)
    y = y.astype(F32)
    y_ids = iota((NY, LANES), 0).astype(F32).astype(BF16)
    right = []
    for brick in range(BAND):
        spread = jnp.broadcast_to(y[brick : brick + 1], (NY, LANES)).astype(BF16)
        right.append(jnp.where(y_ids == spread, constant(1.0), constant(0.0)))
    hot = jnp.concatenate(right, axis=1)
    picked = dot(high_table, hot) + dot(low_table, hot)
    out = []
    for brick in range(BAND):
        part = picked[:, brick * LANES : (brick + 1) * LANES].reshape(ROWS // 8, 8, LANES)
        mine = jnp.broadcast_to(row[brick : brick + 1], (8, LANES))
        for bit in (7, 6, 5, 4, 3):
            half = part.shape[0] // 2
            part = jnp.where(bit_of(mine, bit)[None], part[half:], part[:half])
        hit = iota((8, LANES), 0) == (mine & 7)
        out.append(jnp.sum(jnp.where(hit, part[0], 0.0), axis=0, keepdims=True))
    return jnp.concatenate(out, axis=0)


def look_lanes(table, code):
    row, y = decode(code)
    lane, second = y % LANES, y >= LANES

    def pick(values):
        return jnp.take_along_axis(jnp.broadcast_to(values, (BAND, LANES)), lane, axis=1)

    def tree(start, size):
        if size == 1:
            values = table[start // WIDTH, start % WIDTH : start % WIDTH + 1, :]
            return jnp.where(second, pick(values[:, LANES:]), pick(values[:, :LANES]))
        half = size // 2
        return jnp.where(
            bit_of(row, half.bit_length() - 1), tree(start + half, half), tree(start, half)
        )

    return tree(0, ROWS)


SIDE = 4
MESH = pl.DeviceIdType.MESH
WIDE_PEERS = [1, 2, 3]
DEEP_PEERS = [SIDE, 2 * SIDE, 3 * SIDE]
HOPS = [0, 1, 2, 1]
FAR_FIRST = sorted(range(1, SLABS), key=lambda p: -(HOPS[p // SIDE] + HOPS[p % SIDE]))


def prepare(velocity, plane, column, count, send, slot, me):
    used = used_mask(count[...])
    speed = velocity[...]
    kinetic = 0.5 * (speed[0] * speed[0] + speed[1] * speed[1] + speed[2] * speed[2])
    kinetic = jnp.where(used, kinetic, 0.0)
    planes = plane[...]
    columns = column[...]
    owner = planes[:, 0:1] // PLANES
    place = (owner // SIDE - me // SIDE + SIDE) % SIDE * SIDE + (owner % SIDE - me % SIDE + SIDE) % SIDE
    square = (BRICKS, LANES)
    hits = jnp.where(iota(square, 1) == place, 1.0, 0.0)
    earlier = jnp.where(iota(square, 0) > iota(square, 1), 1.0, 0.0).astype(BF16)
    before = dot(earlier, hits.astype(BF16))
    rank = jnp.sum(before * hits, axis=1, keepdims=True)
    brick_slot = place.astype(F32) * SLOTS + rank
    slot[...] = jnp.broadcast_to(brick_slot, square)
    slot_row = jnp.sum(
        jnp.where(iota(square, 0) == iota(square, 1), brick_slot, 0.0), axis=0, keepdims=True
    )
    slots = SLABS * SLOTS
    pick = jnp.where(iota((slots, BRICKS), 0).astype(F32) == slot_row, 1.0, 0.0).astype(BF16)
    row_code = (planes - owner * PLANES) * WIDTH + columns // NY + 1
    row_code = jnp.where(used, row_code, 0).astype(F32).astype(BF16)
    y_code = jnp.where(used, columns % NY, 0).astype(F32).astype(BF16)
    code = 256.0 * dot(pick, row_code) + dot(pick, y_code)
    high, middle, low = split3(kinetic)
    sent = (dot(pick, high) + dot(pick, middle)) + dot(pick, low)
    send[:, 0] = sent.reshape(SLABS, SLOTS, LANES)
    send[:, 1] = code.reshape(SLABS, SLOTS, LANES)


def eliminate(temp, below, left, right, slab, energies, counts, reduced, fixed, to_low, to_high):
    has_below = jnp.where(slab > 0, 1.0, 0.0)
    shape = (WIDTH, NY)
    lower = has_below * (STIFFNESS * (0.5 * (temp[0] + below[...])))
    ground = current = link = back_ground = back_current = None
    for p in range(PLANES):
        here = temp[p]
        energy = energies[p * WIDTH : (p + 1) * WIDTH]
        count = counts[p * WIDTH : (p + 1) * WIDTH]
        x_less = jnp.concatenate([left[p : p + 1], here[:-1]], axis=0)
        x_more = jnp.concatenate([here[1:], right[p : p + 1]], axis=0)
        y_less = pltpu.roll(here, 1, 1)
        y_more = pltpu.roll(here, NY - 1, 1)
        lateral = LATERAL * (x_less + x_more + y_less + y_more - 4.0 * here)
        excess = here + COUPLE * count
        source = here * here + lateral + (COUPLE * TWO_THIRDS) * energy
        if p == 0:
            link, ground, current = lower, excess, source
            back_ground = back_current = jnp.zeros(shape, F32)
        else:
            upper = STIFFNESS * (0.5 * (temp[p - 1] + here))
            inverse = 1.0 / (ground + link + upper)
            high = upper * inverse
            low = link * inverse
            fixed[p - 1] = current * inverse
            to_low[p - 1] = low
            to_high[p - 1] = high
            back_ground = back_ground + low * ground
            back_current = back_current + low * current
            link = high * link
            ground = excess + high * ground
            current = source + high * current
    for place, value in enumerate([link, ground, current, back_ground, back_current]):
        reduced[:, place, :] = value


def solve_reduced(systems, ends):
    link, ground, current, back_ground, back_current = [systems[:, place, :] for place in range(5)]
    ground = ground + shift_rows(back_ground, 1)
    current = current + shift_rows(back_current, 1)
    below = link
    above = shift_rows(link, 1)
    distance = 1
    while distance < SLABS:
        inverse = 1.0 / (ground + below + above)
        ratio_below = below * shift_rows(inverse, -distance)
        ratio_above = above * shift_rows(inverse, distance)
        ground, current, below, above = (
            ground
            + ratio_below * shift_rows(ground, -distance)
            + ratio_above * shift_rows(ground, distance),
            current
            + ratio_below * shift_rows(current, -distance)
            + ratio_above * shift_rows(current, distance),
            ratio_below * shift_rows(below, -distance),
            ratio_above * shift_rows(above, distance),
        )
        distance *= 2
    value = current / ground
    ends[:, 0, :] = shift_rows(value, -1)
    ends[:, 1, :] = value


def substitute(fixed, to_low, to_high, ends, solved, high_table, low_table):
    low_end = ends[:, 0, :]
    value = ends[:, 1, :]
    for p in range(PLANES - 1, -1, -1):
        if p < PLANES - 1:
            value = (fixed[p] + to_low[p] * low_end) + to_high[p] * value
        solved[p] = value
        high, low = split2(value)
        high_table[p * WIDTH : (p + 1) * WIDTH] = high
        low_table[p * WIDTH : (p + 1) * WIDTH] = low


def kick(velocity, noise, count, slot, returned, moved):
    used = used_mask(count[...])
    slots = SLABS * SLOTS
    slot_ids = iota((BRICKS, slots), 1).astype(F32)
    where_from = jnp.concatenate([slot[...], slot[...]], axis=1)
    pick = jnp.where(slot_ids == where_from, 1.0, 0.0).astype(BF16)
    high, middle, low = split3(returned[...].reshape(slots, LANES))
    temp = (dot(pick, high) + dot(pick, middle)) + dot(pick, low)
    scale = jnp.sqrt(2.0 * KICK_RATE * temp)
    for axis in range(3):
        kicked = (1.0 - KICK_RATE) * velocity[axis] + scale * noise[axis]
        moved[axis] = jnp.where(used, kicked, 0.0)


def step_kernel(
    velocity_in, noise_in, plane_in, column_in, count_in, temp_in,
    solved, moved,
    velocity, noise, plane, column, count, temp,
    send, got, slot, edges, below, sides, energies, counts, reduced, systems, ends, own_ends,
    fixed, to_low, to_high, high_table, low_table, reply, returned,
    row_ready, load_sem, halo_send, halo_recv,
    atom_send, atom_recv, system_send, system_recv, end_send, end_recv, reply_send, reply_recv,
):
    me = lax.axis_index("gz")
    line = lax.axis_index("gx")
    lines = lax.axis_size("gx")
    next_line = lax.rem(line + 1, lines)
    last_line = lax.rem(line + lines - 1, lines)
    deep, wide = me // SIDE, me % SIDE

    def ahead(place):
        return (deep + place // SIDE) % SIDE * SIDE + (wide + place % SIDE) % SIDE

    def behind(place):
        return (deep + SIDE - place // SIDE) % SIDE * SIDE + (wide + SIDE - place % SIDE) % SIDE

    def remote(source, target, sent, received, where):
        return pltpu.make_async_remote_copy(
            src_ref=source, dst_ref=target, send_sem=sent, recv_sem=received,
            device_id=where, device_id_type=MESH,
        )

    loads = [
        pltpu.make_async_copy(source, target, load_sem.at[place])
        for place, (source, target) in enumerate(
            [
                (plane_in, plane),
                (column_in, column),
                (count_in, count),
                (velocity_in, velocity),
                (temp_in, temp),
                (noise_in, noise),
            ]
        )
    ]
    for load in loads:
        load.start()
    barrier = pltpu.get_barrier_semaphore()
    for place in WIDE_PEERS + DEEP_PEERS:
        pl.semaphore_signal(barrier, inc=1, device_id={"gz": ahead(place)}, device_id_type=MESH)
    for where in (next_line, last_line):
        pl.semaphore_signal(barrier, inc=1, device_id={"gx": where}, device_id_type=MESH)
    for load in loads[:4]:
        load.wait()
    prepare(velocity, plane, column, count, send, slot, me)
    bin_group([(send[0, 0], send[0, 1])], energies, counts, True)
    pl.semaphore_wait(barrier, len(WIDE_PEERS + DEEP_PEERS) + 2)

    def atoms(place):
        return remote(
            send.at[place], got.at[place], atom_send.at[place], atom_recv.at[place], {"gz": ahead(place)}
        )

    for place in DEEP_PEERS:
        pl.semaphore_signal(row_ready, inc=1, device_id={"gz": ahead(place)}, device_id_type=MESH)
    for place in WIDE_PEERS + DEEP_PEERS:
        atoms(place).start()
    loads[4].wait()
    edges[0] = temp[:, 0, :]
    edges[1] = temp[:, WIDTH - 1, :]
    halos = [
        remote(temp.at[PLANES - 1], below, halo_send.at[0], halo_recv.at[0], {"gz": (me + 1) % SLABS}),
        remote(edges.at[1], sides.at[0], halo_send.at[1], halo_recv.at[1], {"gx": next_line}),
        remote(edges.at[0], sides.at[1], halo_send.at[2], halo_recv.at[2], {"gx": last_line}),
    ]
    for halo in halos[1:]:
        halo.start()
    pl.semaphore_wait(row_ready, len(DEEP_PEERS))
    for place in range(SIDE, SLABS):
        if place % SIDE:
            atoms(place).start()
    halos[0].start()

    def bin_places(places):
        for place in places:
            atoms(place).wait_recv()
        bin_group([(got[place, 0], got[place, 1]) for place in places], energies, counts, False)

    bin_places(range(1, SIDE))

    def bin_turn(turn, carry):
        bin_places([turn * SIDE + i for i in range(SIDE)])
        return carry

    lax.fori_loop(1, SIDE, bin_turn, 0)
    for halo in halos:
        halo.wait_recv()
    eliminate(temp, below, sides.at[0], sides.at[1], me, energies, counts, reduced, fixed, to_low, to_high)

    def system(place):
        return remote(
            reduced.at[ahead(place)], systems.at[me], system_send.at[place], system_recv.at[place],
            {"gz": ahead(place)},
        )

    for place in FAR_FIRST:
        system(place).start()
    systems[me] = reduced[me]
    for place in range(1, SLABS):
        system(place).wait_recv()
    solve_reduced(systems, ends)

    def end(place):
        return remote(
            ends.at[ahead(place)], own_ends.at[me], end_send.at[place], end_recv.at[place],
            {"gz": ahead(place)},
        )

    for place in FAR_FIRST:
        end(place).start()
    own_ends[me] = ends[me]
    for place in range(1, SLABS):
        end(place).wait_recv()
    substitute(fixed, to_low, to_high, own_ends, solved, high_table, low_table)

    def answer(place):
        return remote(
            reply.at[place], returned.at[place], reply_send.at[place], reply_recv.at[place],
            {"gz": behind(place)},
        )

    def look_places(places, target):
        bands = [(source, place, band) for source, place in places for band in (0, BAND)]
        values = []
        for number, (source, place, band) in enumerate(bands):
            code = source[place, 1][band : band + BAND]
            if number * 8 < len(bands) * 5:
                values.append(look_product(high_table[...], low_table[...], code))
            else:
                values.append(look_lanes(solved, code))
        for (_, place, band), value in zip(bands, values):
            target[place, band : band + BAND] = value

    def look_turn(turn, carry):
        places = [(SIDE - 1 - turn) * SIDE + i for i in range(SIDE)]
        look_places([(got, place) for place in places], reply)
        for place in places:
            answer(place).start()
        return carry

    lax.fori_loop(0, SIDE - 1, look_turn, 0)
    look_places([(got, place) for place in range(1, SIDE)], reply)
    for place in range(1, SIDE):
        answer(place).start()
    look_places([(send, 0)], returned)
    loads[5].wait()
    for place in range(1, SLABS):
        answer(place).wait_recv()
    kick(velocity, noise, count, slot, returned, moved)
    for halo in halos:
        halo.wait_send()
    for place in range(1, SLABS):
        atoms(place).wait_send()
        system(place).wait_send()
        end(place).wait_send()
        answer(place).wait_send()


def store_kernel(solved, moved, solved_out, moved_out, sems):
    copies = [
        pltpu.make_async_copy(solved, solved_out, sems.at[0]),
        pltpu.make_async_copy(moved, moved_out, sems.at[1]),
    ]
    for copy in copies:
        copy.start()
    for copy in copies:
        copy.wait()


def shape(*dims):
    return jax.ShapeDtypeStruct(dims, F32)


def body(velocity, noise, plane, column, brick_count, temp):
    count = brick_count.reshape(1, BRICKS)
    vmem = pltpu.VMEM
    inner = vmem((PLANES - 1, WIDTH, NY), F32)
    chunk = vmem((SLABS, 2, SLOTS, LANES), F32)
    line = vmem((SLABS, SLOTS, LANES), F32)
    table = vmem((ROWS, NY), BF16)
    pairs = pltpu.SemaphoreType.DMA((SLABS,))
    outs = (shape(PLANES, WIDTH, NY), shape(3, BRICKS, LANES))
    solved, moved = pl.pallas_call(
        step_kernel,
        out_shape=(vmem((PLANES, WIDTH, NY), F32), vmem((3, BRICKS, LANES), F32)),
        in_specs=[pl.BlockSpec(memory_space=pl.ANY)] * 6,
        out_specs=(pl.BlockSpec(memory_space=pltpu.VMEM),) * 2,
        scratch_shapes=[
            vmem((3, BRICKS, LANES), F32),
            vmem((3, BRICKS, LANES), F32),
            vmem((BRICKS, LANES), jnp.int32),
            vmem((BRICKS, LANES), jnp.int32),
            vmem((1, BRICKS), jnp.int32),
            vmem((PLANES, WIDTH, NY), F32),
            chunk,
            chunk,
            vmem((BRICKS, LANES), F32),
            vmem((2, PLANES, NY), F32),
            vmem((WIDTH, NY), F32),
            vmem((2, PLANES, NY), F32),
            vmem((ROWS, NY), F32),
            vmem((ROWS, NY), F32),
            vmem((WIDTH, 5, NY), F32),
            vmem((SLABS, 5, NY), F32),
            vmem((SLABS, 2, NY), F32),
            vmem((WIDTH, 2, NY), F32),
            inner,
            inner,
            inner,
            table,
            table,
            line,
            line,
            pltpu.SemaphoreType.REGULAR,
            pltpu.SemaphoreType.DMA((6,)),
            pltpu.SemaphoreType.DMA((3,)),
            pltpu.SemaphoreType.DMA((3,)),
        ]
        + [pairs] * 8,
        compiler_params=pltpu.CompilerParams(collective_id=0, has_side_effects=True),
    )(velocity, noise, plane, column, count, temp)
    return pl.pallas_call(
        store_kernel,
        out_shape=outs,
        in_specs=[pl.BlockSpec(memory_space=pltpu.VMEM)] * 2,
        out_specs=(pl.BlockSpec(memory_space=pl.ANY),) * 2,
        scratch_shapes=[pltpu.SemaphoreType.DMA((2,))],
    )(*[pltpu.with_memory_space_constraint(value, pltpu.VMEM) for value in (solved, moved)])


def solution(mesh):
    placed = (
        P(None, ("gz", "gx"), None),
        P(None, ("gz", "gx"), None),
        P(("gz", "gx"), None),
        P(("gz", "gx"), None),
        P(("gz", "gx")),
        P("gz", "gx", None),
    )
    return jax.shard_map(
        body,
        mesh=mesh,
        in_specs=placed,
        out_specs=(P("gz", "gx", None), P(None, ("gz", "gx"), None)),
        check_vma=False,
    )
```

```python
import jax
import jax.numpy as jnp
from jax import lax
from jax.experimental import pallas as pl
from jax.experimental.pallas import tpu as pltpu
from jax.sharding import PartitionSpec as P

STIFFNESS = 10000.0
LATERAL = 0.1
COUPLE = 0.5
TWO_THIRDS = 2.0 / 3.0
KICK_RATE = 0.2
SLABS = 16
PLANES = 16
WIDTH = 16
NY = 256
SLOTS = 16
BRICKS = 128
LANES = 128
F32 = jnp.float32
BF16 = jnp.bfloat16
VMEM = pl.BlockSpec(memory_space=pltpu.VMEM)


def iota(shape, axis):
    return lax.broadcasted_iota(jnp.int32, shape, axis)


def split3(value):
    high = value.astype(BF16)
    rest = value - high.astype(F32)
    middle = rest.astype(BF16)
    low = (rest - middle.astype(F32)).astype(BF16)
    return high, middle, low


def split2(value):
    high = value.astype(BF16)
    low = (value - high.astype(F32)).astype(BF16)
    return high, low


def dot(a, b, contract=((1,), (0,))):
    return lax.dot_general(a, b, (contract, ((), ())), preferred_element_type=F32)


def used_mask(count_row):
    diagonal = iota((BRICKS, LANES), 0) == iota((BRICKS, LANES), 1)
    count_column = jnp.sum(jnp.where(diagonal, count_row.astype(F32), 0.0), axis=1, keepdims=True)
    return iota((BRICKS, LANES), 1).astype(F32) < count_column


ROWS = PLANES * WIDTH


F8 = jnp.float8_e4m3fn
LOW_SCALE = 4096.0


def decode(code):
    whole = code.astype(jnp.int32)
    return whole // 256 - 1, whole % 256


def constant(value):
    return jnp.full((), value, BF16)


def bin_chunk(kinetic, code):
    row, y = decode(code)
    row, y = row.astype(F32), y.astype(F32)
    high = kinetic.astype(BF16).astype(F32)
    low = (kinetic - high) * LOW_SCALE
    ids = iota((ROWS, LANES), 0).astype(F32).astype(BF16)
    one, zero = constant(1.0), constant(0.0)
    left, left_low, right = [], [], []
    for brick in range(SLOTS):

        def spread(value):
            return jnp.broadcast_to(value[brick : brick + 1], (ROWS, LANES)).astype(BF16)

        hit = ids == spread(row)
        left.append(jnp.where(hit, spread(high), zero))
        left_low.append(
            jnp.concatenate(
                [
                    jnp.where(hit, spread(low), zero).astype(F8),
                    jnp.where(hit, one, zero).astype(F8),
                ],
                axis=0,
            )
        )
        right.append(jnp.where(ids == spread(y), one, zero))
    last = ((1,), (1,))
    upper = dot(jnp.concatenate(left, axis=1), jnp.concatenate(right, axis=1), contract=last)
    right_low = jnp.concatenate([value.astype(F8) for value in right], axis=1)
    rest = dot(jnp.concatenate(left_low, axis=1), right_low, contract=last)
    return upper + rest[:ROWS] * (1.0 / LOW_SCALE), rest[ROWS:]


def add_up(values):
    while len(values) > 1:
        values = [sum(values[i : i + 2]) for i in range(0, len(values), 2)]
    return values[0]


def bin_group(chunks, energy, counts, first):
    parts = [bin_chunk(kinetic, code) for kinetic, code in chunks]
    for target, values in zip((energy, counts), zip(*parts)):
        value = add_up(list(values))
        target[...] = value if first else target[...] + value


def shift_rows(value, step):
    zeros = jnp.zeros((abs(step), value.shape[1]), value.dtype)
    if step > 0:
        return jnp.concatenate([value[step:], zeros], axis=0)
    return jnp.concatenate([zeros, value[:step]], axis=0)


BAND = 8


def bit_of(value, bit):
    return ((value >> bit) & 1) == 1


def look_product(high_table, low_table, code):
    row, y = decode(code)
    y = y.astype(F32)
    y_ids = iota((NY, LANES), 0).astype(F32).astype(BF16)
    right = []
    for brick in range(BAND):
        spread = jnp.broadcast_to(y[brick : brick + 1], (NY, LANES)).astype(BF16)
        right.append(jnp.where(y_ids == spread, constant(1.0), constant(0.0)))
    hot = jnp.concatenate(right, axis=1)
    picked = dot(high_table, hot) + dot(low_table, hot)
    tables = []
    for start in range(0, picked.shape[0], ROWS):
        out = []
        for brick in range(BAND):
            lanes = slice(brick * LANES, (brick + 1) * LANES)
            part = picked[start : start + ROWS, lanes].reshape(ROWS // 8, 8, LANES)
            mine = jnp.broadcast_to(row[brick : brick + 1], (8, LANES))
            for bit in (7, 6, 5, 4, 3):
                half = part.shape[0] // 2
                part = jnp.where(bit_of(mine, bit)[None], part[half:], part[:half])
            hit = iota((8, LANES), 0) == (mine & 7)
            out.append(jnp.sum(jnp.where(hit, part[0], 0.0), axis=0, keepdims=True))
        tables.append(jnp.concatenate(out, axis=0))
    return tables


def look_ends(ends, code):
    row, y = decode(code)
    lane, second = y % LANES, y >= LANES

    def pick(values):
        return jnp.take_along_axis(jnp.broadcast_to(values, (BAND, LANES)), lane, axis=1)

    def tree(end, start, size):
        if size == 1:
            values = ends[start, end : end + 1, :]
            return jnp.where(second, pick(values[:, LANES:]), pick(values[:, :LANES]))
        half = size // 2
        return jnp.where(
            bit_of(row, half.bit_length() - 1), tree(end, start + half, half), tree(end, start, half)
        )

    return tree(0, 0, WIDTH), tree(1, 0, WIDTH)


def look_lanes(table, code):
    row, y = decode(code)
    lane, second = y % LANES, y >= LANES

    def pick(values):
        return jnp.take_along_axis(jnp.broadcast_to(values, (BAND, LANES)), lane, axis=1)

    def tree(start, size):
        if size == 1:
            values = table[start // WIDTH, start % WIDTH : start % WIDTH + 1, :]
            return jnp.where(second, pick(values[:, LANES:]), pick(values[:, :LANES]))
        half = size // 2
        return jnp.where(
            bit_of(row, half.bit_length() - 1), tree(start + half, half), tree(start, half)
        )

    return tree(0, ROWS)


SIDE = 4
MESH = pl.DeviceIdType.MESH
WIDE_PEERS = [1, 2, 3]
DEEP_PEERS = [SIDE, 2 * SIDE, 3 * SIDE]
HOPS = [0, 1, 2, 1]
EARLY = [12, 13, 14, 15]
FAR_FIRST = sorted(range(1, SLABS), key=lambda p: -(HOPS[p // SIDE] + HOPS[p % SIDE]))


def prepare(velocity, plane, column, count, send, slot, me):
    used = used_mask(count[...])
    speed = velocity[...]
    kinetic = 0.5 * (speed[0] * speed[0] + speed[1] * speed[1] + speed[2] * speed[2])
    kinetic = jnp.where(used, kinetic, 0.0)
    planes = plane[...]
    columns = column[...]
    owner = planes[:, 0:1] // PLANES
    place = (owner // SIDE - me // SIDE + SIDE) % SIDE * SIDE + (owner % SIDE - me % SIDE + SIDE) % SIDE
    square = (BRICKS, LANES)
    hits = jnp.where(iota(square, 1) == place, 1.0, 0.0)
    earlier = jnp.where(iota(square, 0) > iota(square, 1), 1.0, 0.0).astype(BF16)
    before = dot(earlier, hits.astype(BF16))
    rank = jnp.sum(before * hits, axis=1, keepdims=True)
    brick_slot = place.astype(F32) * SLOTS + rank
    slot[...] = jnp.broadcast_to(brick_slot, square)
    slot_row = jnp.sum(
        jnp.where(iota(square, 0) == iota(square, 1), brick_slot, 0.0), axis=0, keepdims=True
    )
    slots = SLABS * SLOTS
    pick = jnp.where(iota((slots, BRICKS), 0).astype(F32) == slot_row, 1.0, 0.0).astype(BF16)
    row_code = (planes - owner * PLANES) * WIDTH + columns // NY + 1
    row_code = jnp.where(used, row_code, 0).astype(F32).astype(BF16)
    y_code = jnp.where(used, columns % NY, 0).astype(F32).astype(BF16)
    code = 256.0 * dot(pick, row_code) + dot(pick, y_code)
    high, middle, low = split3(kinetic)
    sent = (dot(pick, high) + dot(pick, middle)) + dot(pick, low)
    send[:, 0] = sent.reshape(SLABS, SLOTS, LANES)
    send[:, 1] = code.reshape(SLABS, SLOTS, LANES)


def eliminate(temp, below, left, right, slab, energies, counts, reduced, fixed, to_low, to_high):
    has_below = jnp.where(slab > 0, 1.0, 0.0)
    shape = (WIDTH, NY)
    lower = has_below * (STIFFNESS * (0.5 * (temp[0] + below[...])))
    ground = current = link = back_ground = back_current = None
    for p in range(PLANES):
        here = temp[p]
        energy = energies[p * WIDTH : (p + 1) * WIDTH]
        count = counts[p * WIDTH : (p + 1) * WIDTH]
        x_less = jnp.concatenate([left[p : p + 1], here[:-1]], axis=0)
        x_more = jnp.concatenate([here[1:], right[p : p + 1]], axis=0)
        y_less = pltpu.roll(here, 1, 1)
        y_more = pltpu.roll(here, NY - 1, 1)
        lateral = LATERAL * (x_less + x_more + y_less + y_more - 4.0 * here)
        excess = here + COUPLE * count
        source = here * here + lateral + (COUPLE * TWO_THIRDS) * energy
        if p == 0:
            link, ground, current = lower, excess, source
            back_ground = back_current = jnp.zeros(shape, F32)
        else:
            upper = STIFFNESS * (0.5 * (temp[p - 1] + here))
            inverse = 1.0 / (ground + link + upper)
            high = upper * inverse
            low = link * inverse
            fixed[p - 1] = current * inverse
            to_low[p - 1] = low
            to_high[p - 1] = high
            back_ground = back_ground + low * ground
            back_current = back_current + low * current
            link = high * link
            ground = excess + high * ground
            current = source + high * current
    for place, value in enumerate([link, ground, current, back_ground, back_current]):
        reduced[:, place, :] = value


def solve_reduced(systems, ends):
    link, ground, current, back_ground, back_current = [systems[:, place, :] for place in range(5)]
    ground = ground + shift_rows(back_ground, 1)
    current = current + shift_rows(back_current, 1)
    below = link
    above = shift_rows(link, 1)
    distance = 1
    while distance < SLABS:
        inverse = 1.0 / (ground + below + above)
        ratio_below = below * shift_rows(inverse, -distance)
        ratio_above = above * shift_rows(inverse, distance)
        ground, current, below, above = (
            ground
            + ratio_below * shift_rows(ground, -distance)
            + ratio_above * shift_rows(ground, distance),
            current
            + ratio_below * shift_rows(current, -distance)
            + ratio_above * shift_rows(current, distance),
            ratio_below * shift_rows(below, -distance),
            ratio_above * shift_rows(above, distance),
        )
        distance *= 2
    value = current / ground
    ends[:, 0, :] = shift_rows(value, -1)
    ends[:, 1, :] = value


def compose(fixed, to_low, to_high, high_parts, low_parts):
    shape = (WIDTH, NY)
    values = [jnp.zeros(shape, F32), jnp.zeros(shape, F32), jnp.ones(shape, F32)]
    for p in range(PLANES - 1, -1, -1):
        if p < PLANES - 1:
            ratio = to_high[p]
            values = [
                fixed[p] + ratio * values[0],
                to_low[p] + ratio * values[1],
                ratio * values[2],
            ]
            fixed[p], to_low[p], to_high[p] = values
        for number, value in enumerate(values):
            rows = slice(number * ROWS + p * WIDTH, number * ROWS + (p + 1) * WIDTH)
            high_parts[rows], low_parts[rows] = split2(value)


def substitute(fixed, to_low, to_high, ends, solved, high_table, low_table):
    low_end = ends[:, 0, :]
    last = ends[:, 1, :]
    for p in range(PLANES):
        value = last
        if p < PLANES - 1:
            value = (fixed[p] + to_low[p] * low_end) + to_high[p] * last
        solved[p] = value
        high, low = split2(value)
        high_table[p * WIDTH : (p + 1) * WIDTH] = high
        low_table[p * WIDTH : (p + 1) * WIDTH] = low


def kick_ready(velocity, count, slot, moved):
    used = used_mask(count[...])
    slot_ids = iota((BRICKS, SLABS * SLOTS), 1).astype(F32)
    where_from = jnp.concatenate([slot[...], slot[...]], axis=1)
    for axis in range(3):
        moved[axis] = jnp.where(used, (1.0 - KICK_RATE) * velocity[axis], 0.0)
    return used, jnp.where(slot_ids == where_from, 1.0, 0.0).astype(BF16)


def kick(noise, used, pick, returned, moved):
    terms = jnp.concatenate(split3(returned[...].reshape(SLABS * SLOTS, LANES)), axis=1)
    sums = dot(pick, terms)
    temp = (sums[:, :LANES] + sums[:, LANES : 2 * LANES]) + sums[:, 2 * LANES :]
    scale = jnp.sqrt(2.0 * KICK_RATE * temp)
    for axis in range(3):
        moved[axis] += jnp.where(used, scale * noise[axis], 0.0)


def step_kernel(
    velocity_in, noise_in, plane_in, column_in, count_in, temp_in,
    solved, moved,
    velocity, noise, plane, column, count, temp,
    send, got, slot, edges, below, sides, energies, counts, reduced, systems, ends, own_ends,
    fixed, to_low, to_high, high_table, low_table, high_parts, low_parts, parts, reply, returned,
    row_ready, load_sem, halo_send, halo_recv,
    atom_send, atom_recv, system_send, system_recv, end_send, end_recv, reply_send, reply_recv,
):
    me = lax.axis_index("gz")
    line = lax.axis_index("gx")
    lines = lax.axis_size("gx")
    next_line = lax.rem(line + 1, lines)
    last_line = lax.rem(line + lines - 1, lines)
    deep, wide = me // SIDE, me % SIDE

    def ahead(place):
        return (deep + place // SIDE) % SIDE * SIDE + (wide + place % SIDE) % SIDE

    def behind(place):
        return (deep + SIDE - place // SIDE) % SIDE * SIDE + (wide + SIDE - place % SIDE) % SIDE

    def remote(source, target, sent, received, where):
        return pltpu.make_async_remote_copy(
            src_ref=source, dst_ref=target, send_sem=sent, recv_sem=received,
            device_id=where, device_id_type=MESH,
        )

    loads = [
        pltpu.make_async_copy(source, target, load_sem.at[place])
        for place, (source, target) in enumerate(
            [
                (plane_in, plane),
                (column_in, column),
                (count_in, count),
                (velocity_in, velocity),
                (temp_in, temp),
                (noise_in, noise),
            ]
        )
    ]
    for load in loads:
        load.start()
    barrier = pltpu.get_barrier_semaphore()
    for place in WIDE_PEERS + DEEP_PEERS:
        pl.semaphore_signal(barrier, inc=1, device_id={"gz": ahead(place)}, device_id_type=MESH)
    for where in (next_line, last_line):
        pl.semaphore_signal(barrier, inc=1, device_id={"gx": where}, device_id_type=MESH)
    for load in loads[:4]:
        load.wait()
    prepare(velocity, plane, column, count, send, slot, me)
    bin_group([(send[0, 0], send[0, 1])], energies, counts, True)
    pl.semaphore_wait(barrier, len(WIDE_PEERS + DEEP_PEERS) + 2)

    def atoms(place):
        return remote(
            send.at[place], got.at[place], atom_send.at[place], atom_recv.at[place], {"gz": ahead(place)}
        )

    for place in DEEP_PEERS:
        pl.semaphore_signal(row_ready, inc=1, device_id={"gz": ahead(place)}, device_id_type=MESH)
    for place in WIDE_PEERS + DEEP_PEERS:
        atoms(place).start()
    loads[4].wait()
    edges[0] = temp[:, 0, :]
    edges[1] = temp[:, WIDTH - 1, :]
    halos = [
        remote(temp.at[PLANES - 1], below, halo_send.at[0], halo_recv.at[0], {"gz": (me + 1) % SLABS}),
        remote(edges.at[1], sides.at[0], halo_send.at[1], halo_recv.at[1], {"gx": next_line}),
        remote(edges.at[0], sides.at[1], halo_send.at[2], halo_recv.at[2], {"gx": last_line}),
    ]
    for halo in halos[1:]:
        halo.start()
    pl.semaphore_wait(row_ready, len(DEEP_PEERS))
    for place in range(SIDE, SLABS):
        if place % SIDE:
            atoms(place).start()
    halos[0].start()

    def bin_places(places):
        for place in places:
            atoms(place).wait_recv()
        bin_group([(got[place, 0], got[place, 1]) for place in places], energies, counts, False)

    bin_places(range(1, SIDE))

    def bin_turn(turn, carry):
        bin_places([turn * SIDE + i for i in range(SIDE)])
        return carry

    lax.fori_loop(1, SIDE, bin_turn, 0)
    for halo in halos:
        halo.wait_recv()
    eliminate(temp, below, sides.at[0], sides.at[1], me, energies, counts, reduced, fixed, to_low, to_high)

    def system(place):
        return remote(
            reduced.at[ahead(place)], systems.at[me], system_send.at[place], system_recv.at[place],
            {"gz": ahead(place)},
        )

    for place in FAR_FIRST:
        system(place).start()
    systems[me] = reduced[me]
    compose(fixed, to_low, to_high, high_parts, low_parts)

    def look_early(places):
        bands = [(place, band) for place in places for band in (0, BAND)]
        values = [
            look_product(high_parts[...], low_parts[...], got[place, 1][band : band + BAND])
            for place, band in bands
        ]
        for (place, band), value in zip(bands, values):
            for number in range(3):
                parts[place - EARLY[0], number, band : band + BAND] = value[number]

    look_early(EARLY[:2])
    for place in range(1, SLABS):
        system(place).wait_recv()
    solve_reduced(systems, ends)

    def end(place):
        return remote(
            ends.at[ahead(place)], own_ends.at[me], end_send.at[place], end_recv.at[place],
            {"gz": ahead(place)},
        )

    for place in FAR_FIRST:
        end(place).start()
    own_ends[me] = ends[me]
    look_early(EARLY[2:])
    for place in range(1, SLABS):
        end(place).wait_recv()
    substitute(fixed, to_low, to_high, own_ends, solved, high_table, low_table)

    def answer(place):
        return remote(
            reply.at[place], returned.at[place], reply_send.at[place], reply_recv.at[place],
            {"gz": behind(place)},
        )

    def finish(place, band):
        rows = slice(band, band + BAND)
        below_end, last = look_ends(own_ends, got[place, 1][rows])
        base, low, high = [parts[place - EARLY[0], number, rows] for number in range(3)]
        return (base + low * below_end) + high * last

    def look_places(places, target, products, early=()):
        bands = [(source, place, band) for source, place in places for band in (0, BAND)]
        ends_of = [(place, band) for place in early for band in (0, BAND)]
        done = [finish(place, band) for place, band in ends_of]
        values = []
        for number, (source, place, band) in enumerate(bands):
            code = source[place, 1][band : band + BAND]
            if number < products:
                values.append(look_product(high_table[...], low_table[...], code)[0])
            else:
                values.append(look_lanes(solved, code))
        for (place, band), value in zip(ends_of, done):
            target[place, band : band + BAND] = value
        for (_, place, band), value in zip(bands, values):
            target[place, band : band + BAND] = value

    def look_group(places, products, early=()):
        look_places([(got, place) for place in places], reply, products, early)
        for place in [*early, *places]:
            answer(place).start()

    look_group(range(8, 12), 6, EARLY)
    look_group(range(4, 8), 5)
    look_group(range(1, 4), 4)
    look_places([(send, 0)], returned, 2)
    loads[5].wait()
    used, pick = kick_ready(velocity, count, slot, moved)
    for place in range(1, SLABS):
        answer(place).wait_recv()
    kick(noise, used, pick, returned, moved)
    for halo in halos:
        halo.wait_send()
    for place in range(1, SLABS):
        atoms(place).wait_send()
        system(place).wait_send()
        end(place).wait_send()
        answer(place).wait_send()


def store_kernel(solved, moved, solved_out, moved_out, sems):
    copies = [
        pltpu.make_async_copy(solved, solved_out, sems.at[0]),
        pltpu.make_async_copy(moved, moved_out, sems.at[1]),
    ]
    for copy in copies:
        copy.start()
    for copy in copies:
        copy.wait()


def shape(*dims):
    return jax.ShapeDtypeStruct(dims, F32)


def body(velocity, noise, plane, column, brick_count, temp):
    count = brick_count.reshape(1, BRICKS)
    vmem = pltpu.VMEM
    inner = vmem((PLANES - 1, WIDTH, NY), F32)
    chunk = vmem((SLABS, 2, SLOTS, LANES), F32)
    line = vmem((SLABS, SLOTS, LANES), F32)
    table = vmem((ROWS, NY), BF16)
    pairs = pltpu.SemaphoreType.DMA((SLABS,))
    outs = (shape(PLANES, WIDTH, NY), shape(3, BRICKS, LANES))
    solved, moved = pl.pallas_call(
        step_kernel,
        out_shape=(vmem((PLANES, WIDTH, NY), F32), vmem((3, BRICKS, LANES), F32)),
        in_specs=[pl.BlockSpec(memory_space=pl.ANY)] * 6,
        out_specs=(pl.BlockSpec(memory_space=pltpu.VMEM),) * 2,
        scratch_shapes=[
            vmem((3, BRICKS, LANES), F32),
            vmem((3, BRICKS, LANES), F32),
            vmem((BRICKS, LANES), jnp.int32),
            vmem((BRICKS, LANES), jnp.int32),
            vmem((1, BRICKS), jnp.int32),
            vmem((PLANES, WIDTH, NY), F32),
            chunk,
            chunk,
            vmem((BRICKS, LANES), F32),
            vmem((2, PLANES, NY), F32),
            vmem((WIDTH, NY), F32),
            vmem((2, PLANES, NY), F32),
            vmem((ROWS, NY), F32),
            vmem((ROWS, NY), F32),
            vmem((WIDTH, 5, NY), F32),
            vmem((SLABS, 5, NY), F32),
            vmem((SLABS, 2, NY), F32),
            vmem((WIDTH, 2, NY), F32),
            inner,
            inner,
            inner,
            table,
            table,
            vmem((3 * ROWS, NY), BF16),
            vmem((3 * ROWS, NY), BF16),
            vmem((len(EARLY), 3, SLOTS, LANES), F32),
            line,
            line,
            pltpu.SemaphoreType.REGULAR,
            pltpu.SemaphoreType.DMA((6,)),
            pltpu.SemaphoreType.DMA((3,)),
            pltpu.SemaphoreType.DMA((3,)),
        ]
        + [pairs] * 8,
        compiler_params=pltpu.CompilerParams(collective_id=0, has_side_effects=True),
    )(velocity, noise, plane, column, count, temp)
    return pl.pallas_call(
        store_kernel,
        out_shape=outs,
        in_specs=[pl.BlockSpec(memory_space=pltpu.VMEM)] * 2,
        out_specs=(pl.BlockSpec(memory_space=pl.ANY),) * 2,
        scratch_shapes=[pltpu.SemaphoreType.DMA((2,))],
    )(*[pltpu.with_memory_space_constraint(value, pltpu.VMEM) for value in (solved, moved)])


def solution(mesh):
    placed = (
        P(None, ("gz", "gx"), None),
        P(None, ("gz", "gx"), None),
        P(("gz", "gx"), None),
        P(("gz", "gx"), None),
        P(("gz", "gx")),
        P("gz", "gx", None),
    )
    return jax.shard_map(
        body,
        mesh=mesh,
        in_specs=placed,
        out_specs=(P("gz", "gx", None), P(None, ("gz", "gx"), None)),
        check_vma=False,
    )
```

```python
import jax
import jax.numpy as jnp
from jax import lax
from jax.experimental import pallas as pl
from jax.experimental.pallas import tpu as pltpu
from jax.sharding import PartitionSpec as P

STIFFNESS = 10000.0
LATERAL = 0.1
COUPLE = 0.5
TWO_THIRDS = 2.0 / 3.0
KICK_RATE = 0.2
SLABS = 16
PLANES = 16
WIDTH = 16
NY = 256
SLOTS = 16
BRICKS = 128
LANES = 128
F32 = jnp.float32
BF16 = jnp.bfloat16
VMEM = pl.BlockSpec(memory_space=pltpu.VMEM)


def iota(shape, axis):
    return lax.broadcasted_iota(jnp.int32, shape, axis)


def split3(value):
    high = value.astype(BF16)
    rest = value - high.astype(F32)
    middle = rest.astype(BF16)
    low = (rest - middle.astype(F32)).astype(BF16)
    return high, middle, low


def split2(value):
    high = value.astype(BF16)
    low = (value - high.astype(F32)).astype(BF16)
    return high, low


def dot(a, b, contract=((1,), (0,))):
    return lax.dot_general(a, b, (contract, ((), ())), preferred_element_type=F32)


def used_mask(count_row):
    diagonal = iota((BRICKS, LANES), 0) == iota((BRICKS, LANES), 1)
    count_column = jnp.sum(jnp.where(diagonal, count_row.astype(F32), 0.0), axis=1, keepdims=True)
    return iota((BRICKS, LANES), 1).astype(F32) < count_column


ROWS = PLANES * WIDTH


F8 = jnp.float8_e4m3fn
LOW_SCALE = 4096.0


def decode(code):
    whole = code.astype(jnp.int32)
    return whole // 256 - 1, whole % 256


def constant(value):
    return jnp.full((), value, BF16)


def bin_chunk(kinetic, code):
    row, y = decode(code)
    row, y = row.astype(F32), y.astype(F32)
    high = kinetic.astype(BF16).astype(F32)
    low = (kinetic - high) * LOW_SCALE
    ids = iota((ROWS, LANES), 0).astype(F32).astype(BF16)
    one, zero = constant(1.0), constant(0.0)
    left, left_low, right = [], [], []
    for brick in range(SLOTS):

        def spread(value):
            return jnp.broadcast_to(value[brick : brick + 1], (ROWS, LANES)).astype(BF16)

        hit = ids == spread(row)
        left.append(jnp.where(hit, spread(high), zero))
        left_low.append(
            jnp.concatenate(
                [
                    jnp.where(hit, spread(low), zero).astype(F8),
                    jnp.where(hit, one, zero).astype(F8),
                ],
                axis=0,
            )
        )
        right.append(jnp.where(ids == spread(y), one, zero))
    last = ((1,), (1,))
    upper = dot(jnp.concatenate(left, axis=1), jnp.concatenate(right, axis=1), contract=last)
    right_low = jnp.concatenate([value.astype(F8) for value in right], axis=1)
    rest = dot(jnp.concatenate(left_low, axis=1), right_low, contract=last)
    return upper + rest[:ROWS] * (1.0 / LOW_SCALE), rest[ROWS:]


def add_up(values):
    while len(values) > 1:
        values = [sum(values[i : i + 2]) for i in range(0, len(values), 2)]
    return values[0]


def bin_group(chunks, energy, counts, first):
    parts = [bin_chunk(kinetic, code) for kinetic, code in chunks]
    for target, values in zip((energy, counts), zip(*parts)):
        value = add_up(list(values))
        target[...] = value if first else target[...] + value


def shift_rows(value, step):
    zeros = jnp.zeros((abs(step), value.shape[1]), value.dtype)
    if step > 0:
        return jnp.concatenate([value[step:], zeros], axis=0)
    return jnp.concatenate([zeros, value[:step]], axis=0)


BAND = 8


def bit_of(value, bit):
    return ((value >> bit) & 1) == 1


def look_product(high_table, low_table, code):
    row, y = decode(code)
    y = y.astype(F32)
    y_ids = iota((NY, LANES), 0).astype(F32).astype(BF16)
    right = []
    for brick in range(BAND):
        spread = jnp.broadcast_to(y[brick : brick + 1], (NY, LANES)).astype(BF16)
        right.append(jnp.where(y_ids == spread, constant(1.0), constant(0.0)))
    hot = jnp.concatenate(right, axis=1)
    picked = dot(high_table, hot) + dot(low_table, hot)
    tables = []
    for start in range(0, picked.shape[0], ROWS):
        out = []
        for brick in range(BAND):
            lanes = slice(brick * LANES, (brick + 1) * LANES)
            part = picked[start : start + ROWS, lanes].reshape(ROWS // 8, 8, LANES)
            mine = jnp.broadcast_to(row[brick : brick + 1], (8, LANES))
            for bit in (7, 6, 5, 4, 3):
                half = part.shape[0] // 2
                part = jnp.where(bit_of(mine, bit)[None], part[half:], part[:half])
            hit = iota((8, LANES), 0) == (mine & 7)
            out.append(jnp.sum(jnp.where(hit, part[0], 0.0), axis=0, keepdims=True))
        tables.append(jnp.concatenate(out, axis=0))
    return tables


def look_ends(ends, code):
    row, y = decode(code)
    lane, second = y % LANES, y >= LANES

    def pick(values):
        return jnp.take_along_axis(jnp.broadcast_to(values, (BAND, LANES)), lane, axis=1)

    def tree(end, start, size):
        if size == 1:
            values = ends[start, end : end + 1, :]
            return jnp.where(second, pick(values[:, LANES:]), pick(values[:, :LANES]))
        half = size // 2
        return jnp.where(
            bit_of(row, half.bit_length() - 1), tree(end, start + half, half), tree(end, start, half)
        )

    return tree(0, 0, WIDTH), tree(1, 0, WIDTH)


def look_lanes(table, code):
    row, y = decode(code)
    lane, second = y % LANES, y >= LANES

    def pick(values):
        return jnp.take_along_axis(jnp.broadcast_to(values, (BAND, LANES)), lane, axis=1)

    def tree(start, size):
        if size == 1:
            values = table[start // WIDTH, start % WIDTH : start % WIDTH + 1, :]
            return jnp.where(second, pick(values[:, LANES:]), pick(values[:, :LANES]))
        half = size // 2
        return jnp.where(
            bit_of(row, half.bit_length() - 1), tree(start + half, half), tree(start, half)
        )

    return tree(0, ROWS)


SIDE = 4
MESH = pl.DeviceIdType.MESH
WIDE_PEERS = [1, 2, 3]
DEEP_PEERS = [SIDE, 2 * SIDE, 3 * SIDE]
HOPS = [0, 1, 2, 1]
EARLY = [12, 13, 14, 15]
FAR_FIRST = sorted(range(1, SLABS), key=lambda p: -(HOPS[p // SIDE] + HOPS[p % SIDE]))


def prepare(velocity, plane, column, count, send, slot, me):
    used = used_mask(count[...])
    speed = velocity[...]
    kinetic = 0.5 * (speed[0] * speed[0] + speed[1] * speed[1] + speed[2] * speed[2])
    kinetic = jnp.where(used, kinetic, 0.0)
    planes = plane[...]
    columns = column[...]
    owner = planes[:, 0:1] // PLANES
    place = (owner // SIDE - me // SIDE + SIDE) % SIDE * SIDE + (owner % SIDE - me % SIDE + SIDE) % SIDE
    square = (BRICKS, LANES)
    hits = jnp.where(iota(square, 1) == place, 1.0, 0.0)
    earlier = jnp.where(iota(square, 0) > iota(square, 1), 1.0, 0.0).astype(BF16)
    before = dot(earlier, hits.astype(BF16))
    rank = jnp.sum(before * hits, axis=1, keepdims=True)
    brick_slot = place.astype(F32) * SLOTS + rank
    slot[...] = jnp.broadcast_to(brick_slot, square)
    slot_row = jnp.sum(
        jnp.where(iota(square, 0) == iota(square, 1), brick_slot, 0.0), axis=0, keepdims=True
    )
    slots = SLABS * SLOTS
    pick = jnp.where(iota((slots, BRICKS), 0).astype(F32) == slot_row, 1.0, 0.0).astype(BF16)
    row_code = (planes - owner * PLANES) * WIDTH + columns // NY + 1
    row_code = jnp.where(used, row_code, 0).astype(F32).astype(BF16)
    y_code = jnp.where(used, columns % NY, 0).astype(F32).astype(BF16)
    code = 256.0 * dot(pick, row_code) + dot(pick, y_code)
    high, middle, low = split3(kinetic)
    sent = (dot(pick, high) + dot(pick, middle)) + dot(pick, low)
    send[:, 0] = sent.reshape(SLABS, SLOTS, LANES)
    send[:, 1] = code.reshape(SLABS, SLOTS, LANES)


def eliminate(temp, below, left, right, slab, energies, counts, reduced, fixed, to_low, to_high):
    has_below = jnp.where(slab > 0, 1.0, 0.0)
    shape = (WIDTH, NY)
    lower = has_below * (STIFFNESS * (0.5 * (temp[0] + below[...])))
    ground = current = link = back_ground = back_current = None
    for p in range(PLANES):
        here = temp[p]
        energy = energies[p * WIDTH : (p + 1) * WIDTH]
        count = counts[p * WIDTH : (p + 1) * WIDTH]
        x_less = jnp.concatenate([left[p : p + 1], here[:-1]], axis=0)
        x_more = jnp.concatenate([here[1:], right[p : p + 1]], axis=0)
        y_less = pltpu.roll(here, 1, 1)
        y_more = pltpu.roll(here, NY - 1, 1)
        lateral = LATERAL * (x_less + x_more + y_less + y_more - 4.0 * here)
        excess = here + COUPLE * count
        source = here * here + lateral + (COUPLE * TWO_THIRDS) * energy
        if p == 0:
            link, ground, current = lower, excess, source
            back_ground = back_current = jnp.zeros(shape, F32)
        else:
            upper = STIFFNESS * (0.5 * (temp[p - 1] + here))
            inverse = 1.0 / (ground + link + upper)
            high = upper * inverse
            low = link * inverse
            fixed[p - 1] = current * inverse
            to_low[p - 1] = low
            to_high[p - 1] = high
            back_ground = back_ground + low * ground
            back_current = back_current + low * current
            link = high * link
            ground = excess + high * ground
            current = source + high * current
    for place, value in enumerate([link, ground, current, back_ground, back_current]):
        reduced[:, place, :] = value


def solve_reduced(systems, ends):
    link, ground, current, back_ground, back_current = [systems[:, place, :] for place in range(5)]
    ground = ground + shift_rows(back_ground, 1)
    current = current + shift_rows(back_current, 1)
    below = link
    above = shift_rows(link, 1)
    distance = 1
    while distance < SLABS:
        inverse = 1.0 / (ground + below + above)
        ratio_below = below * shift_rows(inverse, -distance)
        ratio_above = above * shift_rows(inverse, distance)
        ground, current, below, above = (
            ground
            + ratio_below * shift_rows(ground, -distance)
            + ratio_above * shift_rows(ground, distance),
            current
            + ratio_below * shift_rows(current, -distance)
            + ratio_above * shift_rows(current, distance),
            ratio_below * shift_rows(below, -distance),
            ratio_above * shift_rows(above, distance),
        )
        distance *= 2
    value = current / ground
    ends[:, 0, :] = shift_rows(value, -1)
    ends[:, 1, :] = value


def compose(fixed, to_low, to_high, high_parts, low_parts):
    shape = (WIDTH, NY)
    values = [jnp.zeros(shape, F32), jnp.zeros(shape, F32), jnp.ones(shape, F32)]
    for p in range(PLANES - 1, -1, -1):
        if p < PLANES - 1:
            ratio = to_high[p]
            values = [
                fixed[p] + ratio * values[0],
                to_low[p] + ratio * values[1],
                ratio * values[2],
            ]
            fixed[p], to_low[p], to_high[p] = values
        for number, value in enumerate(values):
            rows = slice(number * ROWS + p * WIDTH, number * ROWS + (p + 1) * WIDTH)
            high_parts[rows], low_parts[rows] = split2(value)


def substitute(fixed, to_low, to_high, ends, solved, high_table, low_table):
    low_end = ends[:, 0, :]
    last = ends[:, 1, :]
    for p in range(PLANES):
        value = last
        if p < PLANES - 1:
            value = (fixed[p] + to_low[p] * low_end) + to_high[p] * last
        solved[p] = value
        high, low = split2(value)
        high_table[p * WIDTH : (p + 1) * WIDTH] = high
        low_table[p * WIDTH : (p + 1) * WIDTH] = low


def kick_ready(velocity, count, slot, moved):
    used = used_mask(count[...])
    slot_ids = iota((BRICKS, SLABS * SLOTS), 1).astype(F32)
    where_from = jnp.concatenate([slot[...], slot[...]], axis=1)
    for axis in range(3):
        moved[axis] = jnp.where(used, (1.0 - KICK_RATE) * velocity[axis], 0.0)
    return used, jnp.where(slot_ids == where_from, 1.0, 0.0).astype(BF16)


def kick(noise, used, pick, returned, moved):
    terms = jnp.concatenate(split3(returned[...].reshape(SLABS * SLOTS, LANES)), axis=1)
    sums = dot(pick, terms)
    temp = (sums[:, :LANES] + sums[:, LANES : 2 * LANES]) + sums[:, 2 * LANES :]
    scale = jnp.sqrt(2.0 * KICK_RATE * temp)
    for axis in range(3):
        moved[axis] += jnp.where(used, scale * noise[axis], 0.0)


def step_kernel(
    velocity_in, noise_in, plane_in, column_in, count_in, temp_in,
    solved, moved,
    velocity, noise, plane, column, count, temp,
    send, got, slot, edges, below, sides, energies, counts, reduced, systems, ends, own_ends,
    fixed, to_low, to_high, high_table, low_table, high_parts, low_parts, parts, reply, returned,
    row_ready, load_sem, halo_send, halo_recv,
    atom_send, atom_recv, system_send, system_recv, end_send, end_recv, reply_send, reply_recv,
):
    me = lax.axis_index("gz")
    line = lax.axis_index("gx")
    lines = lax.axis_size("gx")
    next_line = lax.rem(line + 1, lines)
    last_line = lax.rem(line + lines - 1, lines)
    deep, wide = me // SIDE, me % SIDE

    def ahead(place):
        return (deep + place // SIDE) % SIDE * SIDE + (wide + place % SIDE) % SIDE

    def behind(place):
        return (deep + SIDE - place // SIDE) % SIDE * SIDE + (wide + SIDE - place % SIDE) % SIDE

    def remote(source, target, sent, received, where):
        return pltpu.make_async_remote_copy(
            src_ref=source, dst_ref=target, send_sem=sent, recv_sem=received,
            device_id=where, device_id_type=MESH,
        )

    loads = [
        pltpu.make_async_copy(source, target, load_sem.at[place])
        for place, (source, target) in enumerate(
            [
                (plane_in, plane),
                (column_in, column),
                (count_in, count),
                (velocity_in, velocity),
                (temp_in, temp),
                (noise_in, noise),
            ]
        )
    ]
    for load in loads:
        load.start()
    barrier = pltpu.get_barrier_semaphore()
    for place in WIDE_PEERS + DEEP_PEERS:
        pl.semaphore_signal(barrier, inc=1, device_id={"gz": ahead(place)}, device_id_type=MESH)
    for where in (next_line, last_line):
        pl.semaphore_signal(barrier, inc=1, device_id={"gx": where}, device_id_type=MESH)
    for load in loads[:4]:
        load.wait()
    prepare(velocity, plane, column, count, send, slot, me)
    bin_group([(send[0, 0], send[0, 1])], energies, counts, True)
    pl.semaphore_wait(barrier, len(WIDE_PEERS + DEEP_PEERS) + 2)

    def atoms(place):
        return remote(
            send.at[place], got.at[place], atom_send.at[place], atom_recv.at[place], {"gz": ahead(place)}
        )

    for place in DEEP_PEERS:
        pl.semaphore_signal(row_ready, inc=1, device_id={"gz": ahead(place)}, device_id_type=MESH)
    for place in WIDE_PEERS + DEEP_PEERS:
        atoms(place).start()
    loads[4].wait()
    edges[0] = temp[:, 0, :]
    edges[1] = temp[:, WIDTH - 1, :]
    halos = [
        remote(temp.at[PLANES - 1], below, halo_send.at[0], halo_recv.at[0], {"gz": (me + 1) % SLABS}),
        remote(edges.at[1], sides.at[0], halo_send.at[1], halo_recv.at[1], {"gx": next_line}),
        remote(edges.at[0], sides.at[1], halo_send.at[2], halo_recv.at[2], {"gx": last_line}),
    ]
    for halo in halos[1:]:
        halo.start()
    pl.semaphore_wait(row_ready, len(DEEP_PEERS))
    for place in range(SIDE, SLABS):
        if place % SIDE:
            atoms(place).start()
    halos[0].start()

    def bin_places(places):
        for place in places:
            atoms(place).wait_recv()
        bin_group([(got[place, 0], got[place, 1]) for place in places], energies, counts, False)

    bin_places(range(1, SIDE))

    def bin_turn(turn, carry):
        steps = 1 + 2 * turn - 3 * (turn * (turn - 1) // 2)
        bin_places([steps * SIDE + i for i in range(SIDE)])
        return carry

    lax.fori_loop(0, SIDE - 1, bin_turn, 0)
    for halo in halos:
        halo.wait_recv()
    eliminate(temp, below, sides.at[0], sides.at[1], me, energies, counts, reduced, fixed, to_low, to_high)

    def system(place):
        return remote(
            reduced.at[ahead(place)], systems.at[me], system_send.at[place], system_recv.at[place],
            {"gz": ahead(place)},
        )

    for place in FAR_FIRST:
        system(place).start()
    systems[me] = reduced[me]
    compose(fixed, to_low, to_high, high_parts, low_parts)

    def look_early(places):
        bands = [(place, band) for place in places for band in (0, BAND)]
        values = [
            look_product(high_parts[...], low_parts[...], got[place, 1][band : band + BAND])
            for place, band in bands
        ]
        for (place, band), value in zip(bands, values):
            for number in range(3):
                parts[place - EARLY[0], number, band : band + BAND] = value[number]

    look_early(EARLY[:2])
    for place in range(1, SLABS):
        system(place).wait_recv()
    solve_reduced(systems, ends)

    def end(place):
        return remote(
            ends.at[ahead(place)], own_ends.at[me], end_send.at[place], end_recv.at[place],
            {"gz": ahead(place)},
        )

    for place in FAR_FIRST:
        end(place).start()
    own_ends[me] = ends[me]
    look_early(EARLY[2:])
    for place in range(1, SLABS):
        end(place).wait_recv()
    substitute(fixed, to_low, to_high, own_ends, solved, high_table, low_table)

    def answer(place):
        return remote(
            reply.at[place], returned.at[place], reply_send.at[place], reply_recv.at[place],
            {"gz": behind(place)},
        )

    def finish(place, band):
        rows = slice(band, band + BAND)
        below_end, last = look_ends(own_ends, got[place, 1][rows])
        base, low, high = [parts[place - EARLY[0], number, rows] for number in range(3)]
        return (base + low * below_end) + high * last

    def look_places(places, target, products, early=()):
        bands = [(source, place, band) for source, place in places for band in (0, BAND)]
        ends_of = [(place, band) for place in early for band in (0, BAND)]
        done = [finish(place, band) for place, band in ends_of]
        values = []
        for number, (source, place, band) in enumerate(bands):
            code = source[place, 1][band : band + BAND]
            if number < products:
                values.append(look_product(high_table[...], low_table[...], code)[0])
            else:
                values.append(look_lanes(solved, code))
        for (place, band), value in zip(ends_of, done):
            target[place, band : band + BAND] = value
        for (_, place, band), value in zip(bands, values):
            target[place, band : band + BAND] = value

    def look_group(places, products, early=()):
        look_places([(got, place) for place in places], reply, products, early)
        for place in [*early, *places]:
            answer(place).start()

    look_group(range(8, 12), 6, EARLY)
    look_group(range(4, 8), 5)
    look_group(range(1, 4), 4)
    look_places([(send, 0)], returned, 2)
    loads[5].wait()
    used, pick = kick_ready(velocity, count, slot, moved)
    for place in range(1, SLABS):
        answer(place).wait_recv()
    kick(noise, used, pick, returned, moved)
    for halo in halos:
        halo.wait_send()
    for place in range(1, SLABS):
        atoms(place).wait_send()
        system(place).wait_send()
        end(place).wait_send()
        answer(place).wait_send()


def store_kernel(solved, moved, solved_out, moved_out, sems):
    copies = [
        pltpu.make_async_copy(solved, solved_out, sems.at[0]),
        pltpu.make_async_copy(moved, moved_out, sems.at[1]),
    ]
    for copy in copies:
        copy.start()
    for copy in copies:
        copy.wait()


def shape(*dims):
    return jax.ShapeDtypeStruct(dims, F32)


def body(velocity, noise, plane, column, brick_count, temp):
    count = brick_count.reshape(1, BRICKS)
    vmem = pltpu.VMEM
    inner = vmem((PLANES - 1, WIDTH, NY), F32)
    chunk = vmem((SLABS, 2, SLOTS, LANES), F32)
    line = vmem((SLABS, SLOTS, LANES), F32)
    table = vmem((ROWS, NY), BF16)
    pairs = pltpu.SemaphoreType.DMA((SLABS,))
    outs = (shape(PLANES, WIDTH, NY), shape(3, BRICKS, LANES))
    solved, moved = pl.pallas_call(
        step_kernel,
        out_shape=(vmem((PLANES, WIDTH, NY), F32), vmem((3, BRICKS, LANES), F32)),
        in_specs=[pl.BlockSpec(memory_space=pl.ANY)] * 6,
        out_specs=(pl.BlockSpec(memory_space=pltpu.VMEM),) * 2,
        scratch_shapes=[
            vmem((3, BRICKS, LANES), F32),
            vmem((3, BRICKS, LANES), F32),
            vmem((BRICKS, LANES), jnp.int32),
            vmem((BRICKS, LANES), jnp.int32),
            vmem((1, BRICKS), jnp.int32),
            vmem((PLANES, WIDTH, NY), F32),
            chunk,
            chunk,
            vmem((BRICKS, LANES), F32),
            vmem((2, PLANES, NY), F32),
            vmem((WIDTH, NY), F32),
            vmem((2, PLANES, NY), F32),
            vmem((ROWS, NY), F32),
            vmem((ROWS, NY), F32),
            vmem((WIDTH, 5, NY), F32),
            vmem((SLABS, 5, NY), F32),
            vmem((SLABS, 2, NY), F32),
            vmem((WIDTH, 2, NY), F32),
            inner,
            inner,
            inner,
            table,
            table,
            vmem((3 * ROWS, NY), BF16),
            vmem((3 * ROWS, NY), BF16),
            vmem((len(EARLY), 3, SLOTS, LANES), F32),
            line,
            line,
            pltpu.SemaphoreType.REGULAR,
            pltpu.SemaphoreType.DMA((6,)),
            pltpu.SemaphoreType.DMA((3,)),
            pltpu.SemaphoreType.DMA((3,)),
        ]
        + [pairs] * 8,
        compiler_params=pltpu.CompilerParams(collective_id=0, has_side_effects=True),
    )(velocity, noise, plane, column, count, temp)
    return pl.pallas_call(
        store_kernel,
        out_shape=outs,
        in_specs=[pl.BlockSpec(memory_space=pltpu.VMEM)] * 2,
        out_specs=(pl.BlockSpec(memory_space=pl.ANY),) * 2,
        scratch_shapes=[pltpu.SemaphoreType.DMA((2,))],
    )(*[pltpu.with_memory_space_constraint(value, pltpu.VMEM) for value in (solved, moved)])


def solution(mesh):
    placed = (
        P(None, ("gz", "gx"), None),
        P(None, ("gz", "gx"), None),
        P(("gz", "gx"), None),
        P(("gz", "gx"), None),
        P(("gz", "gx")),
        P("gz", "gx", None),
    )
    return jax.shard_map(
        body,
        mesh=mesh,
        in_specs=placed,
        out_specs=(P("gz", "gx", None), P(None, ("gz", "gx"), None)),
        check_vma=False,
    )
```
